32 devices in a mesh: groups: 2 (over x), dp: 4 (over z), tensor: 4 (over y, core).
Axes of the slice: x: 2, y: 2, z: 4, core: 2. Of those that a mesh axis runs over, the one named last changes fastest.
Arguments:
- patches: float32 [16, 256, 6144], P(('groups', 'dp'), None, 'tensor'), parts along dimension 0, may hold values from -60 to 60
- counts: int32 [16], P(('groups', 'dp')), parts along dimension 0, may hold values from 1 to 63, as said below
- ranking: int32 [16, 256], P(('groups', 'dp')), parts along dimension 0, may hold values from 0 to 255, each once within a row
- norm_gain: float32 [6144], P('tensor'), may hold values from 0.1 to 1.9
- expand_weight: bfloat16 [24576, 6144], P(('dp', 'tensor')), may hold values from -0.078125 to 0.078125
- expand_bias: bfloat16 [24576], P(('dp', 'tensor')), may hold values from -4 to 4
- reduce_weight: bfloat16 [24576, 6144], P(('dp', 'tensor')), may hold values from -0.078125 to 0.078125
- reduce_bias: float32 [6144], P('tensor'), may hold values from -4 to 4
Outputs:
- updated: float32 [16, 256, 6144], P(('groups', 'dp'), None, 'tensor'), parts along dimension 0
The draws below stay inside these ranges and needn't reach their ends.
There are 2 independent parts, one for each index of `groups`. The reference program is written for one: setup_inputs(seed, part) draws one part's arguments, and reference() takes and returns one part's arrays. A program takes and returns all parts, laid end to end along the dimension named above; an argument that names none is the same for every part. Nothing has to cross between parts.
Inputs may be any that keep to these rules, and one draw needn't show every extreme that they name: The counts of the 2 images of one index of dp (images b * 2 to (b + 1) * 2 - 1) sum to at most 64; in every draw one such group sums to exactly 64, and some image holds exactly 63.
All inputs are finite; a program needn't handle non-finite values.
Results may differ from the reference program's by a relative error of at most 0.00061.
Values may be sent and summed in bfloat16 or wider, within the bound.
A program may use at most 128 MiB of HBM per device.

```python
import jax
import jax.numpy as jnp
from jax import lax

D = 6144
FF = 24576
PATCH = 256
IMG_DEV = 2
CAP = 64
IMAGES = 8


def draw_patches(key, part):
    key_base, key_rows, key_cols = jax.random.split(key, 3)
    ramp = 1.0 + 2.0 * jnp.arange(D, dtype=jnp.float32) / D
    cols = jnp.exp(jax.random.uniform(key_cols, (1, 1, D), jnp.float32, jnp.log(0.5), jnp.log(1.5))) * ramp
    base = jnp.clip(jax.random.normal(key_base, (IMAGES, PATCH, D), jnp.float32), -4.0, 4.0)
    rows = jnp.exp(jax.random.uniform(key_rows, (IMAGES, PATCH, 1), jnp.float32, jnp.log(0.3), jnp.log(3.0)))
    return base * rows * cols


def draw_counts(key, part):
    key_total, key_full, key_share = jax.random.split(jax.random.fold_in(key, 17), 3)
    blocks = IMAGES // IMG_DEV
    totals = jax.random.randint(key_total, (blocks,), IMG_DEV, CAP + 1)
    full = jax.random.randint(key_full, (), 0, blocks)
    totals = jnp.where(jnp.arange(blocks) == full, CAP, totals)
    shares = jax.random.randint(key_share, (blocks, IMG_DEV), 1, 100)
    extra = totals - IMG_DEV
    pieces = 1 + extra[:, None] * shares // jnp.sum(shares, axis=1, keepdims=True)
    rest = totals - jnp.sum(pieces, axis=1)
    pieces = pieces.at[:, 0].add(rest)
    lopsided = jnp.where(jnp.arange(IMG_DEV) == 0, CAP - IMG_DEV + 1, 1)
    pieces = jnp.where((jnp.arange(blocks) == full)[:, None], lopsided[None, :], pieces)
    return pieces.reshape(IMAGES).astype(jnp.int32)


def levels(key, extent, cuts, least, high):
    gain, own = 1.0, jax.random.fold_in(key, 6)
    for position, blocks in cuts:
        steps = jnp.exp(jax.random.uniform(jax.random.fold_in(own, position), (blocks,), jnp.float32, least / len(cuts), high / len(cuts)))
        gain = gain * jnp.repeat(steps, extent[position] // blocks).reshape([-1 if axis == position else 1 for axis in range(len(extent))])
    return gain


def noise(rng, dims, spread, most, cuts=(), kind=jnp.bfloat16):
    loudness = levels(rng, dims, cuts, -0.22, 0.18) if cuts else 1.0
    drawn = jax.random.normal(rng, dims, jnp.float32) * spread * loudness
    return jnp.minimum(jnp.maximum(drawn, -most), most).astype(kind)


def setup_inputs(seed: int = 0, part: int = 0) -> dict:
    seeds = jax.random.split(jax.random.key(seed), 9)
    part_keys = jax.random.split(jax.random.fold_in(seeds[8], part), 9)
    return {
        "patches": draw_patches(jax.random.fold_in(jax.random.fold_in(seeds[8], part), 71), part),
        "counts": draw_counts(jax.random.fold_in(jax.random.fold_in(seeds[8], part), 71), part),
        "ranking": jax.vmap(lambda own: jax.random.permutation(own, PATCH))(jax.random.split(part_keys[2], IMAGES)).reshape((IMAGES, PATCH)).astype(jnp.int32),
        "norm_gain": jnp.clip(1.0 + 0.18 * jax.random.normal(seeds[3], (D,), jnp.float32), 0.1, 1.9),
        "expand_weight": noise(seeds[4], (FF, D), D ** -0.5, 0.078125, ((0, 16),)),
        "expand_bias": noise(seeds[5], (FF,), 0.7, 4.0, ((0, 16),)),
        "reduce_weight": noise(seeds[6], (FF, D), (FF // 4) ** -0.5, 0.078125, ((0, 16),)),
        "reduce_bias": noise(seeds[7], (D,), 0.7, 4.0, ((0, 4),), jnp.float32),
    }


def reference(patches, counts, ranking, norm_gain, expand_weight, expand_bias, reduce_weight, reduce_bias):
    chosen = ranking[:, :CAP].astype(jnp.int32)
    live = jnp.arange(CAP, dtype=jnp.int32)[None, :] < counts[:, None]
    rows = jnp.take_along_axis(patches, chosen[:, :, None], axis=1)
    flat = rows.reshape(IMAGES * CAP, D)
    first = lax.optimization_barrier(jnp.sum(flat, axis=1, keepdims=True))
    second = lax.optimization_barrier(jnp.sum(flat * flat, axis=1, keepdims=True))
    mean = first / D
    var = second / D - mean * mean
    normed = ((flat - mean) * lax.rsqrt(var + 1e-06) * norm_gain).astype(jnp.bfloat16)
    pre = lax.dot_general(normed, expand_weight, (((1,), (1,)), ((), ())), preferred_element_type=jnp.float32)
    pre = pre + expand_bias.astype(jnp.float32)
    hidden = jax.nn.gelu(pre, approximate=True).astype(jnp.bfloat16)
    branch = jnp.dot(hidden, reduce_weight, preferred_element_type=jnp.float32)
    update = flat + (branch + reduce_bias)
    update = jnp.where(live.reshape(IMAGES * CAP)[:, None], update, flat).reshape(IMAGES, CAP, D)
    image_index = jnp.arange(IMAGES, dtype=jnp.int32)[:, None]
    return patches.at[image_index, chosen].set(update)
```

```python
import functools

import jax
import jax.numpy as jnp
from jax import lax
from jax.experimental import pallas as pl
from jax.experimental.pallas import tpu as pltpu
from jax.sharding import PartitionSpec as P

CAP = 64
MESH = pl.DeviceIdType.MESH


def block_kernel(
    Z, T, C, C2, counts, ranking, ranking_v, gain, ebias, rbias, flat, e_hbm, r_hbm, pt,
    rows, pick,    xg, wv, rv, pre, hid, bias, last, st, cs, cr, own, ys, yr, zs, zr,
    psem, wsem, rsem, st_s, st_r, za_s, za_r, ya_s, ya_r, ca_s, ca_r,
    cr_s, cr_r, yr_s, yr_r, zr_s, zr_r,
):
    Y = T // 2
    R, dl = rows.shape
    images, patch_len = ranking.shape
    N = images * patch_len
    hl, D = e_hbm.shape
    M, dlc, w2 = Z * R, dl // C, dl // C2
    nt = 256 if hl % 256 == 0 else hl
    z = lax.axis_index("dp")
    t = lax.axis_index("tensor")
    y, c = t // 2, t % 2
    z_next = lax.rem(z + 1, Z)
    t_next = lax.rem(y + 1, Y) * 2 + c
    t_part = y * 2 + 1 - c

    barrier = pltpu.get_barrier_semaphore()
    for k in range(1, Z):
        pl.semaphore_signal(barrier, inc=1, device_id={"dp": lax.rem(z + k, Z)}, device_id_type=MESH)
    for k in range(1, T):
        pl.semaphore_signal(barrier, inc=1, device_id={"tensor": lax.rem(t + k, T)}, device_id_type=MESH)

    def copy(src, dst, ss, rs, axis, index):
        return pltpu.make_async_remote_copy(
            src_ref=src, dst_ref=dst, send_sem=ss, recv_sem=rs,
            device_id={axis: index}, device_id_type=MESH,
        )

    def t_of(u, core):
        return lax.rem(y - u + Y, Y) * 2 + core

    def t_red(u, core):
        return lax.rem(y - 1 - u + 2 * Y, Y) * 2 + core

    order = []
    for u in range(Y):
        for core in (c, 1 - c):
            for p in range(C):
                order.append((t_of(u, core), p))

    def expand_load(i):
        block, p = order[i]
        lanes = pl.ds(pl.multiple_of(block * dl + p * dlc, 128), dlc)
        return pltpu.make_async_copy(e_hbm.at[:, lanes], wv.at[i], wsem.at[i])

    def reduce_load(i):
        block = t_red(i // 2, c if i % 2 == 0 else 1 - c)
        lanes = pl.ds(pl.multiple_of(block * dl, 128), dl)
        return pltpu.make_async_copy(r_hbm.at[:, lanes], rv.at[i], rsem.at[i])

    patch_load = pltpu.make_async_copy(flat, pt, psem)
    patch_load.start()

    lane_w = images * R
    which = lax.broadcasted_iota(jnp.int32, (1, lane_w), 1)
    rank, owner = jnp.full((1, lane_w), -1, jnp.int32), jnp.full((1, lane_w), -1, jnp.int32)
    start = 0
    for i in range(images):
        k = which - i * R
        live = (k >= 0) & (k < counts[i])
        owner = jnp.where(live, start + k, owner)
        start = start + counts[i]
        known = jnp.concatenate([ranking_v[i : i + 1, :R]] * images, axis=1)
        rank = jnp.where(live, i * patch_len + known, rank)
    chosen = jnp.where(lax.broadcasted_iota(jnp.int32, (N, lane_w), 0) == rank, 1.0, 0.0)
    slot = jnp.where(lax.broadcasted_iota(jnp.int32, (R, lane_w), 0) == owner, 1.0, 0.0)
    pick[...] = lax.dot_general(
        chosen.astype(jnp.bfloat16), slot.astype(jnp.bfloat16), (((1,), (1,)), ((), ())),
        preferred_element_type=jnp.float32,
    ).astype(jnp.bfloat16)

    def take(j, carry):
        start, source = 0, 0
        for i in range(images):
            offset = j - start
            inside = (offset >= 0) & (offset < counts[i])
            here = i * patch_len + ranking[i, jnp.clip(offset, 0, patch_len - 1)]
            source = jnp.where(inside, here, source)
            start = start + counts[i]
        rows[pl.ds(j, 1), :] = pt[pl.ds(source, 1), :]
        return carry

    patch_load.wait()
    for i in range(T * C):
        expand_load(i).start()
    for i in range(T):
        reduce_load(i).start()
    lax.fori_loop(0, R, take, 0, unroll=8)

    bias[...] = ebias[...].astype(jnp.float32)[None, :]
    x = rows[...]
    s1 = jnp.sum(x, axis=1, keepdims=True)
    s2 = jnp.sum(x * x, axis=1, keepdims=True)
    lane = lax.broadcasted_iota(jnp.int32, (R, 128), 1)
    st[t] = jnp.where(lane == 0, s1, s2)
    pl.semaphore_wait(barrier, Z + T - 2)

    def stat_copy(k):
        return copy(st.at[t], st.at[t], st_s.at[k - 1], st_r.at[k - 1], "tensor", lax.rem(t + k, T))

    for k in range(1, T):
        stat_copy(k).start()
    for k in range(1, T):
        stat_copy(k).wait_recv()
    total = st[0]
    for k in range(1, T):
        total = total + st[k]
    gain_row = gain[...][None, :]
    mean = total[:, 0:1] / D
    var = total[:, 1:2] / D - mean * mean
    scale = lax.rsqrt(var + 1e-06)
    mine = pl.ds(pl.multiple_of(z * R, R), R)
    for p in range(C):
        cols = slice(p * dlc, (p + 1) * dlc)
        xg[t, p, mine, :] = ((rows[:, cols] - mean) * scale * gain_row[:, cols]).astype(jnp.bfloat16)

    def block(tt, j, p):
        return xg.at[tt, p, pl.ds(pl.multiple_of(lax.rem(z - j + Z, Z) * R, R), R), :]

    def z_copy(s, p):
        b = block(t, s - 1, p)
        return copy(b, b, za_s.at[s - 1, p], za_r.at[s - 1, p], "dp", z_next)

    def y_copy(u, j, p):
        b = block(t_of(u - 1, c), j, p)
        return copy(b, b, ya_s.at[u - 1, j, p], ya_r.at[u - 1, j, p], "tensor", t_next)

    def c_copy(u, j, p):
        b = block(t_of(u, c), j, p)
        return copy(b, b, ca_s.at[u, j, p], ca_r.at[u, j, p], "tensor", t_part)

    def expand(i):
        tt, p = order[i]
        expand_load(i).wait()

        acc = lax.dot_general(
            wv[i], xg[tt, p], (((1,), (1,)), ((), ())), preferred_element_type=jnp.float32
        )
        pre[...] = acc if i == 0 else pre[...] + acc

    def expand_partner(u, p):
        for j in range(Z):
            c_copy(u, j, p).wait_recv()
        expand((2 * u + 1) * C + p)

    def y_arrived(u, j, p):
        y_copy(u, j, p).wait_recv()
        if u < Y - 1:
            y_copy(u + 1, j, p).start()
        c_copy(u, j, p).start()

    for p in range(C):
        z_copy(1, p).start()
        y_copy(1, 0, p).start()
        c_copy(0, 0, p).start()
    for s in range(1, Z):
        for p in range(C):
            z_copy(s, p).wait_recv()
            if s < Z - 1:
                z_copy(s + 1, p).start()
            y_copy(1, s, p).start()
            c_copy(0, s, p).start()
            if s == Z - 1:
                expand(p)
        for p in range(C):
            y_arrived(1, s - 1, p)
    for p in range(C):
        expand_partner(0, p)
    for u in range(1, Y):
        for j in range(Z - 1 if u == 1 else 0, Z):
            for p in range(C):
                y_arrived(u, j, p)
                if j == Z - 1:
                    expand(2 * u * C + p)
                    if p > 0:
                        expand_partner(u, p - 1)
        expand_partner(u, C - 1)

    def activate(n):
        units = slice(None) if nt == hl else pl.ds(pl.multiple_of(n * nt, nt), nt)
        v = pre[units, :].T + bias[:, units]
        hid[:, units] = jax.nn.gelu(v, approximate=True).astype(jnp.bfloat16)

    if nt == hl:
        activate(0)
    else:
        lax.fori_loop(0, hl // nt, lambda n, a: (activate(n), a)[1], 0)

    def cr_copy(u, p):
        return copy(cs.at[u, p], cr.at[u, p], cr_s.at[u, p], cr_r.at[u, p], "tensor", t_part)

    def yr_copy(u, p, h):
        half = slice(h * M // 2, (h + 1) * M // 2)
        return copy(
            ys.at[u - 1, p, half, :], yr.at[u - 1, p, half, :],
            yr_s.at[u - 1, p, h], yr_r.at[u - 1, p, h], "tensor", t_next,
        )

    def zr_copy(k, p):
        there = lax.rem(z + k, Z)
        part = pl.ds(pl.multiple_of(there * R, R), R)
        return copy(zs.at[p, part, :], zr.at[k - 1, p], zr_s.at[k - 1, p], zr_r.at[k - 1, p], "dp", there)

    def columns(p):
        return slice(None) if C2 == 1 else pl.ds(pl.multiple_of(p * w2, w2), w2)

    def product(i, p):
        return jnp.dot(hid[...], rv[i, :, columns(p)], preferred_element_type=jnp.float32)

    def produce(u, p):
        cs[u, p] = product(2 * u + 1, p).astype(jnp.bfloat16)
        cr_copy(u, p).start()
        own[u, p] = product(2 * u, p)

    def combine(u, p):
        cr_copy(u, p).wait_recv()
        v = own[u, p] + cr[u, p].astype(jnp.float32)
        if u == 0:
            ys[0, p] = v.astype(jnp.bfloat16)
            for h in range(2):
                yr_copy(1, p, h).start()
        else:
            own[u, p] = v

    def loop(low, high, body):
        lax.fori_loop(low, high, lambda p, a: (body(p), a)[1], 0)

    for u in range(Y):
        reduce_load(2 * u).wait()
        reduce_load(2 * u + 1).wait()
        produce(u, 0)
        if u > 0:
            combine(u - 1, C2 - 1)

        def step(p):
            produce(u, p)
            combine(u, p - 1)

        if C2 > 1:
            loop(1, C2, step)
    combine(Y - 1, C2 - 1)

    for u in range(1, Y):

        def pass_on(p):
            for h in range(2):
                yr_copy(u, p, h).wait_recv()
                half = slice(h * M // 2, (h + 1) * M // 2)
                v = own[u, p, half, :] + yr[u - 1, p, half, :].astype(jnp.float32)
                if u < Y - 1:
                    ys[u, p, half, :] = v.astype(jnp.bfloat16)
                    yr_copy(u + 1, p, h).start()
                else:
                    own[u, p, half, :] = v
                    zs[p, half, :] = v.astype(jnp.bfloat16)
                    for there in range(h * Z // 2, (h + 1) * Z // 2):

                        @pl.when(there != z)
                        def _():
                            zr_copy(lax.rem(there - z + Z, Z), p).start()

        loop(0, C2, pass_on)

    last[...] = rbias[...][None, :]

    def finish(p):
        acc = own[Y - 1, p, mine, :]
        for k in range(1, Z):
            zr_copy(k, p).wait_recv()
            acc = acc + zr[k - 1, p].astype(jnp.float32)
        cols = columns(p)
        add = acc + last[:, cols]
        top = add.astype(jnp.bfloat16)
        rest = add - top.astype(jnp.float32)
        middle = rest.astype(jnp.bfloat16)
        low = (rest - middle.astype(jnp.float32)).astype(jnp.bfloat16)
        spread = jnp.dot(pick[...], low, preferred_element_type=jnp.float32)
        spread = spread + jnp.dot(pick[...], middle, preferred_element_type=jnp.float32)
        spread = spread + jnp.dot(pick[...], top, preferred_element_type=jnp.float32)
        pt[:, cols] = pt[:, cols] + spread


    loop(0, C2, finish)

    for k in range(1, T):
        stat_copy(k).wait_send()
    for p in range(C):
        for s in range(1, Z):
            z_copy(s, p).wait_send()
        for j in range(Z):
            for u in range(1, Y):
                y_copy(u, j, p).wait_send()
            for u in range(Y):
                c_copy(u, j, p).wait_send()

    def drain(p):
        for u in range(Y):
            cr_copy(u, p).wait_send()
        for u in range(1, Y):
            for h in range(2):
                yr_copy(u, p, h).wait_send()
        for k in range(1, Z):
            zr_copy(k, p).wait_send()

    loop(0, C2, drain)


def body(
    Z, T, patches, counts, ranking, norm_gain, expand_weight, expand_bias, reduce_weight, reduce_bias
):
    images, patch_len, dl = patches.shape
    hl, D = expand_weight.shape
    flat = patches.reshape(images * patch_len, dl)
    R, M, Y = CAP, Z * CAP, T // 2
    C = 3 if dl % 768 == 0 else 1
    w2 = 512 if dl % 512 == 0 else dl
    C2 = dl // w2
    dlc = dl // C
    vmem = pl.BlockSpec(memory_space=pltpu.VMEM)
    hbm = pl.BlockSpec(memory_space=pl.ANY)
    bf16, f32 = jnp.bfloat16, jnp.float32
    dma = pltpu.SemaphoreType.DMA
    N = images * patch_len
    smem = pl.BlockSpec(memory_space=pltpu.SMEM)
    result = pl.pallas_call(
        functools.partial(block_kernel, Z, T, C, C2),
        out_shape=pltpu.VMEM((N, dl), f32),
        in_specs=[smem] * 2 + [vmem] * 4 + [hbm] * 3,
        out_specs=vmem,
        scratch_shapes=[
            pltpu.VMEM((R, dl), f32),
            pltpu.VMEM((N, R), bf16),
            pltpu.VMEM((T, C, M, dlc), bf16),
            pltpu.VMEM((T * C, hl, dlc), bf16),
            pltpu.VMEM((T, hl, dl), bf16),
            pltpu.VMEM((hl, M), f32),
            pltpu.VMEM((M, hl), bf16),
            pltpu.VMEM((1, hl), f32),
            pltpu.VMEM((1, dl), f32),
            pltpu.VMEM((T, R, 128), f32),
            pltpu.VMEM((Y, C2, M, w2), bf16),
            pltpu.VMEM((Y, C2, M, w2), bf16),
            pltpu.VMEM((Y, C2, M, w2), f32),
            pltpu.VMEM((Y - 1, C2, M, w2), bf16),
            pltpu.VMEM((Y - 1, C2, M, w2), bf16),
            pltpu.VMEM((C2, M, w2), bf16),
            pltpu.VMEM((Z - 1, C2, R, w2), bf16),
            dma, dma((T * C,)), dma((T,)),
            dma((T - 1,)), dma((T - 1,)),
            dma((Z - 1, C)), dma((Z - 1, C)),
            dma((Y - 1, Z, C)), dma((Y - 1, Z, C)),
            dma((Y, Z, C)), dma((Y, Z, C)),
            dma((Y, C2)), dma((Y, C2)),
            dma((Y - 1, C2, 2)), dma((Y - 1, C2, 2)),
            dma((Z - 1, C2)), dma((Z - 1, C2)),
        ],
        compiler_params=pltpu.CompilerParams(
            collective_id=0, has_side_effects=True, vmem_limit_bytes=63700000
        ),
        name="feed_forward",
    )(
        counts, ranking, ranking, norm_gain, expand_bias, reduce_bias, flat, expand_weight, reduce_weight,
    )
    return result.reshape(images, patch_len, dl)


def solution(mesh):
    placed = (
        P(("groups", "dp"), None, "tensor"),
        P(("groups", "dp")),
        P(("groups", "dp"), None),
        P("tensor"),
        P(("dp", "tensor"), None),
        P(("dp", "tensor")),
        P(("dp", "tensor"), None),
        P("tensor"),
    )
    return jax.shard_map(
        functools.partial(body, mesh.shape["dp"], mesh.shape["tensor"]),
        mesh=mesh,
        in_specs=placed,
        out_specs=P(("groups", "dp"), None, "tensor"),
        check_vma=False,
    )
```

```python
import functools

import jax
import jax.numpy as jnp
from jax import lax
from jax.experimental import pallas as pl
from jax.experimental.pallas import tpu as pltpu
from jax.sharding import PartitionSpec as P

CAP = 64
MESH = pl.DeviceIdType.MESH


def block_kernel(
    Z, T, C, G, C2, NB, counts, ranking, ranking_v, gain, ebias, rbias, flat, e_hbm, r_hbm, pt,
    rows, pick,    xg, wv, rv, pre, hid, last, st, cs, cr, own, ys, yr, zs, zr, zl, yf,
    psem, wsem, rsem, st_s, st_r, za_s, za_r, ya_s, ya_r, ca_s, ca_r,
    cr_s, cr_r, yr_s, yr_r, zr_s, zr_r, zl_r, yf_s, yf_r,
):
    Y = T // 2
    R, dl = rows.shape
    images, patch_len = ranking.shape
    N = images * patch_len
    hl, D = e_hbm.shape
    M, dlc, w2 = Z * R, dl // C, dl // C2
    nt = 256 if hl % 256 == 0 else hl
    z = lax.axis_index("dp")
    t = lax.axis_index("tensor")
    y, c = t // 2, t % 2
    z_next = lax.rem(z + 1, Z)
    t_next = lax.rem(y + 1, Y) * 2 + c
    t_part = y * 2 + 1 - c

    barrier = pltpu.get_barrier_semaphore()
    for k in range(1, Z):
        pl.semaphore_signal(barrier, inc=1, device_id={"dp": lax.rem(z + k, Z)}, device_id_type=MESH)
    for k in range(1, T):
        pl.semaphore_signal(barrier, inc=1, device_id={"tensor": lax.rem(t + k, T)}, device_id_type=MESH)

    def copy(src, dst, ss, rs, axis, index):
        return pltpu.make_async_remote_copy(
            src_ref=src, dst_ref=dst, send_sem=ss, recv_sem=rs,
            device_id={axis: index}, device_id_type=MESH,
        )

    def t_of(u, core):
        return lax.rem(y - u + Y, Y) * 2 + core

    def t_red(u, core):
        return lax.rem(y - 1 - u + 2 * Y, Y) * 2 + core

    def loop(low, high, body):
        lax.fori_loop(low, high, lambda p, a: (body(p), a)[1], 0)

    def expand_load(n):
        q = n // T
        k = n - q * T
        u = k // 2
        core = c + (k - 2 * u) * (1 - 2 * c)
        lanes = pl.ds(pl.multiple_of(t_of(u, core) * dl + q * G * dlc, 128), G * dlc)
        return pltpu.make_async_copy(e_hbm.at[:, lanes], wv.at[n], wsem.at[n])

    def reduce_load(i):
        u = i // 2
        block = t_red(u, c + (i - 2 * u) * (1 - 2 * c))
        lanes = pl.ds(pl.multiple_of(block * dl, 128), dl)
        return pltpu.make_async_copy(r_hbm.at[:, lanes], rv.at[i], rsem.at[i])

    patch_load = pltpu.make_async_copy(flat, pt, psem)
    patch_load.start()

    lane_w = images * R
    which = lax.broadcasted_iota(jnp.int32, (1, lane_w), 1)
    rank, owner = jnp.full((1, lane_w), -1, jnp.int32), jnp.full((1, lane_w), -1, jnp.int32)
    start = 0
    for i in range(images):
        k = which - i * R
        live = (k >= 0) & (k < counts[i])
        owner = jnp.where(live, start + k, owner)
        start = start + counts[i]
        known = jnp.concatenate([ranking_v[i : i + 1, :R]] * images, axis=1)
        rank = jnp.where(live, i * patch_len + known, rank)
    chosen = jnp.where(lax.broadcasted_iota(jnp.int32, (N, lane_w), 0) == rank, 1.0, 0.0)
    slot = jnp.where(lax.broadcasted_iota(jnp.int32, (R, lane_w), 0) == owner, 1.0, 0.0)
    pick[...] = lax.dot_general(
        chosen.astype(jnp.bfloat16), slot.astype(jnp.bfloat16), (((1,), (1,)), ((), ())),
        preferred_element_type=jnp.float32,
    ).astype(jnp.bfloat16)

    def take(j, carry):
        start, source = 0, 0
        for i in range(images):
            offset = j - start
            inside = (offset >= 0) & (offset < counts[i])
            here = i * patch_len + ranking[i, jnp.clip(offset, 0, patch_len - 1)]
            source = jnp.where(inside, here, source)
            start = start + counts[i]
        rows[pl.ds(j, 1), :] = pt[pl.ds(source, 1), :]
        return carry

    patch_load.wait()
    loop(0, C // G * T, lambda n: expand_load(n).start())
    loop(0, T, lambda i: reduce_load(i).start())
    lax.fori_loop(0, R, take, 0, unroll=8)

    pre[...] = jnp.broadcast_to(ebias[...].astype(jnp.float32)[None, :], pre.shape)
    x = rows[...]
    s1 = jnp.sum(x, axis=1, keepdims=True)
    s2 = jnp.sum(x * x, axis=1, keepdims=True)
    place = lax.broadcasted_iota(jnp.int32, (R, 2 * R), 1) - lax.broadcasted_iota(jnp.int32, (R, 2 * R), 0)
    packed = jnp.sum(jnp.where(place == 0, s1, jnp.where(place == R, s2, 0.0)), axis=0, keepdims=True)
    st[t] = jnp.broadcast_to(packed, st.shape[1:])
    pl.semaphore_wait(barrier, Z + T - 2)

    def stat_copy(k):
        return copy(st.at[t], st.at[t], st_s.at[k - 1], st_r.at[k - 1], "tensor", lax.rem(t + k, T))

    for k in range(1, T):
        stat_copy(k).start()
    for k in range(1, T):
        stat_copy(k).wait_recv()
    both = st[0, 0:1, :]
    for k in range(1, T):
        both = both + st[k, 0:1, :]
    total = [
        jnp.sum(jnp.where(place == k * R, both, 0.0), axis=1, keepdims=True) for k in range(2)
    ]
    gain_row = gain[...][None, :]
    mean = total[0] / D
    var = total[1] / D - mean * mean
    scale = lax.rsqrt(var + 1e-06)
    mine = pl.ds(pl.multiple_of(z * R, R), R)
    for p in range(C):
        cols = slice(p * dlc, (p + 1) * dlc)
        xg[t, p, mine, :] = ((rows[:, cols] - mean) * scale * gain_row[:, cols]).astype(jnp.bfloat16)

    def rows_of(tt, p, zb):
        return xg.at[tt, p, pl.ds(pl.multiple_of(zb * R, R), R), :]

    def inside(i):
        return (i >= 0) & (i < Z)

    def z_copy(way, d, p):
        step = 1 - 2 * way
        ref = rows_of(t, p, z - step * (d - 1))
        return copy(ref, ref, za_s.at[way, d - 1, p], za_r.at[way, d - 1, p], "dp", z + step)

    def z_sends(way, d):
        step = 1 - 2 * way
        return inside(z - step * (d - 1)) & inside(z + step)

    def z_wait(way, d, p):
        ref = rows_of(t, p, 0)
        copy(ref, ref, za_s.at[way, d - 1, p], za_r.at[way, d - 1, p], "dp", z_next).wait_recv()

    def y_copy(u, zb, p):
        ref = rows_of(t_of(u - 1, c), p, zb)
        return copy(ref, ref, ya_s.at[u - 1, zb, p], ya_r.at[u - 1, zb, p], "tensor", t_next)

    def c_copy(u, p):
        ref = xg.at[t_of(u, c), p]
        return copy(ref, ref, ca_s.at[u, p], ca_r.at[u, p], "tensor", t_part)

    def z_send(d, p):
        for way in range(2):
            @pl.when(z_sends(way, d))
            def _():
                z_copy(way, d, p).start()

    def z_arrive(d, p):
        for way in range(2):
            step = 1 - 2 * way
            zb = z - step * d

            @pl.when(inside(zb))
            def _():
                z_wait(way, d, p)
                if d < Z - 1:
                    @pl.when(inside(z + step))
                    def _():
                        z_copy(way, d + 1, p).start()

                if Y > 1:
                    y_copy(1, zb, p).start()

    def expand(n):
        q = n // T
        k = n - q * T
        u = k // 2
        tt = t_of(u, c + (k - 2 * u) * (1 - 2 * c))
        pltpu.make_async_copy(e_hbm.at[:, pl.ds(0, G * dlc)], wv.at[n], wsem.at[n]).wait()
        acc = pre[...]
        for g in range(G):
            acc += lax.dot_general(
                xg[tt, q * G + g], wv[n, :, g * dlc : (g + 1) * dlc], (((1,), (1,)), ((), ())),
                preferred_element_type=jnp.float32,
            )
        pre[...] = acc

    def own_sends(p):
        z_send(1, p)
        if Y > 1:
            y_copy(1, z, p).start()

    loop(0, C, own_sends)
    for d in range(1, Z - 1):
        loop(0, C, functools.partial(z_arrive, d))

    Q = C // G
    dots = [(r, q) for r in range(2) for q in range(Q)]
    for u in range(1, Y):
        for q in range(Q + 1):
            dots += [(2 * u, q)] * (q < Q) + [(2 * u + 1, q - 1)] * (q > 0)

    def look(table, i):
        found = table[0]
        for j in range(1, len(table)):
            found = jnp.where(i == j, table[j], found)
        return found

    def step(i):
        r = look([dot[0] for dot in dots], i)
        q = look([dot[1] for dot in dots], i)
        u = r // 2
        odd = r - 2 * u

        @pl.when(r == 0)
        def _():
            for g in range(G):
                if Z > 1:
                    z_arrive(Z - 1, q * G + g)
                c_copy(0, q * G + g).start()

        @pl.when(odd == 1)
        def _():
            for g in range(G):
                c_copy(u, q * G + g).wait_recv()

        @pl.when((odd == 0) & (r > 0))
        def _():
            for g in range(G):
                p = q * G + g
                for zb in range(Z):
                    y_copy(u, zb, p).wait_recv()
                    if Y > 2:
                        @pl.when(u < Y - 1)
                        def _():
                            y_copy(u + 1, zb, p).start()
                c_copy(u, p).start()

        expand(q * T + r)

    loop(0, T * Q, step)

    def activate(n):
        units = slice(None) if nt == hl else pl.ds(pl.multiple_of(n * nt, nt), nt)
        hid[:, units] = jax.nn.gelu(pre[:, units], approximate=True).astype(jnp.bfloat16)

    if nt == hl:
        activate(0)
    else:
        loop(0, hl // nt, activate)

    def cr_copy(i):
        return copy(cs.at[i], cr.at[i], cr_s.at[i], cr_r.at[i], "tensor", t_part)

    def half_of(h):
        return slice(h * M // 2, (h + 1) * M // 2)

    def yr_copy(u, p, h):
        half = half_of(h)
        return copy(
            ys.at[u - 1, p, half, :], yr.at[u - 1, p, half, :],
            yr_s.at[u - 1, p, h], yr_r.at[u - 1, p, h], "tensor", t_next,
        )

    def yf_copy(b):
        return copy(yf.at[0, b], yf.at[1, b], yf_s.at[b], yf_r.at[b], "tensor", t_next)

    def rows_at(i):
        return pl.ds(pl.multiple_of(i * R, R), R)

    def zr_copy(slot, way, k):
        step = 1 - 2 * way
        src = zs.at[slot, rows_at(z + step * k), :]
        if k <= 2:
            dst, sem, there = zr.at[slot, way, k - 1], zr_r.at[slot, way, k - 1], z + step * k
        else:
            dst, sem, there = zl.at[slot, way, k - 3], zl_r.at[slot, way, k - 3], z + step
        return copy(src, dst, zr_s.at[slot, way, k - 1], sem, "dp", there)

    def zr_wait(slot, way, k):
        src = zs.at[slot, rows_at(0), :]
        copy(src, zr.at[slot, way, k - 1], zr_s.at[slot, way, k - 1], zr_r.at[slot, way, k - 1], "dp", z_next).wait_recv()

    def zl_wait(slot, way, k):
        src = zs.at[slot, rows_at(0), :]
        copy(src, zl.at[slot, way, k - 2], zr_s.at[slot, way, k - 1], zl_r.at[slot, way, k - 2], "dp", z_next).wait_recv()

    def z_scatter(slot, h):
        for k in range(Z - 1, 0, -1):
            for way in range(2):
                step = 1 - 2 * way
                to = (z + step * k >= h * Z // 2) & (z + step * k < (h + 1) * Z // 2)
                if 2 <= k < Z - 1:
                    to = to & jnp.logical_not(inside(z - step))

                @pl.when(to)
                def _():
                    zr_copy(slot, way, k).start()

    def z_relay(slot, at):
        for k in range(Z - 2, 1, -1):
            for way in range(2):
                step = 1 - 2 * way

                @pl.when(inside(z - step) & inside(z + step * k))
                def _():
                    zl_wait(slot, way, k)
                    part = rows_at(z + step * k)
                    v = own[at, part, :] + zl[slot, way, k - 2].astype(jnp.float32)
                    zs[slot, part, :] = v.astype(jnp.bfloat16)
                    zr_copy(slot, way, k).start()

    def z_total(slot, at):
        for way in range(2):
            for k in range(1, min(Z - 1, 2) + 1):
                @pl.when(inside(z - (1 - 2 * way) * k))
                def _():
                    zr_wait(slot, way, k)
                    own[at, mine, :] += zr[slot, way, k - 1].astype(jnp.float32)

    def columns(p):
        return slice(None) if C2 == 1 else pl.ds(pl.multiple_of(p * w2, w2), w2)

    NA = C2 - NB
    first = [(0, p) for p in range(NA)]
    if NB:
        rest = [(u, NA + b) for u in range(Y) for b in range(NB)] + [(1, p) for p in range(NA)]
    else:
        rest = [(u, p) for u in range(1, Y) for p in range(NA)]
    order = []
    if NB:
        while first or rest:
            order += first[:1] + rest[:1]
            first, rest = first[1:], rest[1:]
    else:
        order = first + rest
    steps = len(order)

    def chunk(i):
        i = jnp.clip(i, 0, steps - 1)
        return look([o[0] for o in order], i), look([o[1] for o in order], i)

    def slot_of(u, p):
        return jnp.where(u == Y - 1, p, p + NB)

    def scattered(u, p):
        return (u == Y - 1) | (p >= NA)

    def produce(i):
        u, p = chunk(i)
        at = u * C2 + p

        def one(j):
            n = 2 * u + 1 - j
            to = jnp.where(j == 0, Y * C2, at)
            own[to] = jnp.dot(hid[...], rv[n, :, columns(p)], preferred_element_type=jnp.float32)

            @pl.when(j == 0)
            def _():
                cs[at] = own[Y * C2].astype(jnp.bfloat16)
                cr_copy(at).start()

        loop(0, 2, one)

    def combine(i):
        u, p = chunk(i)
        at = u * C2 + p
        cr_copy(at).wait_recv()
        ringed = (u > 0) & (p < NA)
        for h in range(2):
            half = half_of(h)
            own[at, half, :] += cr[at, half, :].astype(jnp.float32)

            @pl.when(ringed)
            def _():
                yr_copy(u, p, h).wait_recv()
                own[at, half, :] += yr[u - 1, p, half, :].astype(jnp.float32)

            @pl.when(scattered(u, p))
            def _():
                zs[slot_of(u, p), half, :] = own[at, half, :].astype(jnp.bfloat16)
                z_scatter(slot_of(u, p), h)

            @pl.when(jnp.logical_not(scattered(u, p)))
            def _():
                ys[u, p, half, :] = own[at, half, :].astype(jnp.bfloat16)
                yr_copy(u + 1, p, h).start()

    def relay(i):
        u, p = chunk(i)

        @pl.when(scattered(u, p))
        def _():
            z_relay(slot_of(u, p), u * C2 + p)

    def cross(b):
        at = NA + b
        z_total(C2 + b, at)
        yf[0, b] = own[at, mine, :].astype(jnp.bfloat16)
        yf_copy(b).start()

    def reduce(i):
        @pl.when(i == 0)
        def _():
            for j in range(T):
                reduce_load(j).wait()

        @pl.when(i < steps)
        def _():
            produce(i)

        @pl.when((i > 0) & (i <= steps))
        def _():
            combine(i - 1)

        if Z > 3:
            @pl.when(i > 3)
            def _():
                relay(i - 4)

        for b in range(NB):
            @pl.when(i == min(order.index((0, NA + b)) + 9, steps + 3))
            def _():
                cross(b)

    loop(0, steps + 4, reduce)

    last[...] = rbias[...][None, :]

    def sent(p):
        for d in range(1, Z):
            for way in range(2):
                @pl.when(z_sends(way, d))
                def _():
                    z_copy(way, d, p).wait_send()

        for u in range(1, Y):
            for zb in range(Z):
                y_copy(u, zb, p).wait_send()
        for u in range(Y):
            c_copy(u, p).wait_send()

    def drain(i):
        u, p = chunk(i)
        cr_copy(u * C2 + p).wait_send()

        @pl.when(jnp.logical_not(scattered(u, p)))
        def _():
            for h in range(2):
                yr_copy(u + 1, p, h).wait_send()

        @pl.when(scattered(u, p))
        def _():
            for k in range(1, Z):
                for way in range(2):
                    @pl.when(inside(z + (1 - 2 * way) * k))
                    def _():
                        zr_copy(slot_of(u, p), way, k).wait_send()

    def finish(i):
        @pl.when(i == C2 - 1)
        def _():
            for k in range(1, T):
                stat_copy(k).wait_send()
            loop(0, C, sent)
            loop(0, steps, drain)
            for b in range(NB):
                yf_copy(b).wait_send()

        p = lax.rem(i + NA, C2)
        at = (Y - 1) * C2 + p
        z_total(p, at)
        for b in range(NB):
            @pl.when(p == NA + b)
            def _():
                yf_copy(b).wait_recv()
                own[at, mine, :] += yf[1, b].astype(jnp.float32)

        cols = columns(p)
        add = own[at, mine, :] + last[:, cols]
        top = add.astype(jnp.bfloat16)
        rest = add - top.astype(jnp.float32)
        middle = rest.astype(jnp.bfloat16)
        low = (rest - middle.astype(jnp.float32)).astype(jnp.bfloat16)
        spread = jnp.dot(pick[...], low, preferred_element_type=jnp.float32)
        spread = spread + jnp.dot(pick[...], middle, preferred_element_type=jnp.float32)
        spread = spread + jnp.dot(pick[...], top, preferred_element_type=jnp.float32)
        pt[:, cols] = pt[:, cols] + spread

    loop(0, C2, finish)


def body(
    Z, T, patches, counts, ranking, norm_gain, expand_weight, expand_bias, reduce_weight, reduce_bias
):
    images, patch_len, dl = patches.shape
    hl, D = expand_weight.shape
    flat = patches.reshape(images * patch_len, dl)
    R, M, Y = CAP, Z * CAP, T // 2
    C = dl // 256 if dl % 256 == 0 else 1
    w2 = 256 if dl % 256 == 0 else dl
    C2 = dl // w2
    G = 2 if C % 2 == 0 else 1
    NB = 1 if Y == 2 and C2 > 4 else 0
    slots = C2 + NB
    dlc = dl // C
    vmem = pl.BlockSpec(memory_space=pltpu.VMEM)
    hbm = pl.BlockSpec(memory_space=pl.ANY)
    bf16, f32 = jnp.bfloat16, jnp.float32
    dma = pltpu.SemaphoreType.DMA
    N = images * patch_len
    smem = pl.BlockSpec(memory_space=pltpu.SMEM)
    result = pl.pallas_call(
        functools.partial(block_kernel, Z, T, C, G, C2, NB),
        out_shape=pltpu.VMEM((N, dl), f32),
        in_specs=[smem] * 2 + [vmem] * 4 + [hbm] * 3,
        out_specs=vmem,
        scratch_shapes=[
            pltpu.VMEM((R, dl), f32),
            pltpu.VMEM((N, R), bf16),
            pltpu.VMEM((T, C, M, dlc), bf16),
            pltpu.VMEM((T * C // G, hl, G * dlc), bf16),
            pltpu.VMEM((T, hl, dl), bf16),
            pltpu.VMEM((M, hl), f32),
            pltpu.VMEM((M, hl), bf16),
            pltpu.VMEM((1, dl), f32),
            pltpu.VMEM((T, 8, 2 * R), f32),
            pltpu.VMEM((Y * C2, M, w2), bf16),
            pltpu.VMEM((Y * C2, M, w2), bf16),
            pltpu.VMEM((Y * C2 + 1, M, w2), f32),
            pltpu.VMEM((Y - 1, C2, M, w2), bf16),
            pltpu.VMEM((Y - 1, C2, M, w2), bf16),
            pltpu.VMEM((slots, M, w2), bf16),
            pltpu.VMEM((slots, 2, 2, R, w2), bf16),
            pltpu.VMEM((slots, 2, max(Z - 3, 1), R, w2), bf16),
            pltpu.VMEM((2, max(NB, 1), R, w2), bf16),
            dma, dma((T * C // G,)), dma((T,)),
            dma((T - 1,)), dma((T - 1,)),
            dma((2, Z - 1, C)), dma((2, Z - 1, C)),
            dma((Y - 1, Z, C)), dma((Y - 1, Z, C)),
            dma((Y, C)), dma((Y, C)),
            dma((Y * C2,)), dma((Y * C2,)),
            dma((Y - 1, C2, 2)), dma((Y - 1, C2, 2)),
            dma((slots, 2, Z - 1)), dma((slots, 2, 2)), dma((slots, 2, max(Z - 3, 1))),
            dma((max(NB, 1),)), dma((max(NB, 1),)),
        ],
        compiler_params=pltpu.CompilerParams(
            collective_id=0, has_side_effects=True, vmem_limit_bytes=63700000
        ),
        name="feed_forward",
    )(
        counts, ranking, ranking, norm_gain, expand_bias, reduce_bias, flat, expand_weight, reduce_weight,
    )
    return result.reshape(images, patch_len, dl)


def solution(mesh):
    placed = (
        P(("groups", "dp"), None, "tensor"),
        P(("groups", "dp")),
        P(("groups", "dp"), None),
        P("tensor"),
        P(("dp", "tensor"), None),
        P(("dp", "tensor")),
        P(("dp", "tensor"), None),
        P("tensor"),
    )
    return jax.shard_map(
        functools.partial(body, mesh.shape["dp"], mesh.shape["tensor"]),
        mesh=mesh,
        in_specs=placed,
        out_specs=P(("groups", "dp"), None, "tensor"),
        check_vma=False,
    )
```

```python
import functools

import jax
import jax.numpy as jnp
from jax import lax
from jax.experimental import pallas as pl
from jax.experimental.pallas import tpu as pltpu
from jax.sharding import PartitionSpec as P

CAP = 64
LAST = 1
MESH = pl.DeviceIdType.MESH


def block_kernel(
    Z, T, C, G, C2, NB, counts, ranking, ranking_v, gain, ebias, rbias, flat, e_hbm, r_hbm, pt,
    rows, pick,    xg, wv, rv, pre, hid, last, st, cs, cr, own, ys, yr, zs, zr, zl, yf,
    psem, wsem, rsem, st_s, st_r, za_s, za_r, ya_s, ya_r, ca_s, ca_r,
    cr_s, cr_r, yr_s, yr_r, zr_s, zr_r, zl_r, yf_s, yf_r,
):
    Y = T // 2
    R, dl = rows.shape
    images, patch_len = ranking.shape
    N = images * patch_len
    hl, D = e_hbm.shape
    M, dlc, w2 = Z * R, dl // C, dl // C2
    nt = 256 if hl % 256 == 0 else hl
    z = lax.axis_index("dp")
    t = lax.axis_index("tensor")
    y, c = t // 2, t % 2
    z_next = lax.rem(z + 1, Z)
    t_next = lax.rem(y + 1, Y) * 2 + c
    t_part = y * 2 + 1 - c

    barrier = pltpu.get_barrier_semaphore()
    for k in range(1, Z):
        pl.semaphore_signal(barrier, inc=1, device_id={"dp": lax.rem(z + k, Z)}, device_id_type=MESH)
    for k in range(1, T):
        pl.semaphore_signal(barrier, inc=1, device_id={"tensor": lax.rem(t + k, T)}, device_id_type=MESH)

    def copy(src, dst, ss, rs, axis, index):
        return pltpu.make_async_remote_copy(
            src_ref=src, dst_ref=dst, send_sem=ss, recv_sem=rs,
            device_id={axis: index}, device_id_type=MESH,
        )

    def t_of(u, core):
        return lax.rem(y - u + Y, Y) * 2 + core

    def t_red(u, core):
        return lax.rem(y - 1 - u + 2 * Y, Y) * 2 + core

    def loop(low, high, body):
        lax.fori_loop(low, high, lambda p, a: (body(p), a)[1], 0)

    def expand_load(n):
        q = n // T
        k = n - q * T
        u = k // 2
        core = c + (k - 2 * u) * (1 - 2 * c)
        lanes = pl.ds(pl.multiple_of(t_of(u, core) * dl + q * G * dlc, 128), G * dlc)
        return pltpu.make_async_copy(e_hbm.at[:, lanes], wv.at[n], wsem.at[q])

    def reduce_load(i):
        u = i // 2
        block = t_red(u, c + (i - 2 * u) * (1 - 2 * c))
        lanes = pl.ds(pl.multiple_of(block * dl, 128), dl)
        return pltpu.make_async_copy(r_hbm.at[:, lanes], rv.at[i], rsem)

    patch_load = pltpu.make_async_copy(flat, pt, psem)
    patch_load.start()

    lane_w = images * R
    which = lax.broadcasted_iota(jnp.int32, (1, lane_w), 1)
    rank, owner = jnp.full((1, lane_w), -1, jnp.int32), jnp.full((1, lane_w), -1, jnp.int32)
    start = 0
    for i in range(images):
        k = which - i * R
        live = (k >= 0) & (k < counts[i])
        owner = jnp.where(live, start + k, owner)
        start = start + counts[i]
        known = jnp.concatenate([ranking_v[i : i + 1, :R]] * images, axis=1)
        rank = jnp.where(live, i * patch_len + known, rank)
    chosen = jnp.where(lax.broadcasted_iota(jnp.int32, (N, lane_w), 0) == rank, 1.0, 0.0)
    slot = jnp.where(lax.broadcasted_iota(jnp.int32, (R, lane_w), 0) == owner, 1.0, 0.0)
    pick[...] = lax.dot_general(
        chosen.astype(jnp.bfloat16), slot.astype(jnp.bfloat16), (((1,), (1,)), ((), ())),
        preferred_element_type=jnp.float32,
    ).astype(jnp.bfloat16)

    def take(j, carry):
        start, source = 0, 0
        for i in range(images):
            offset = j - start
            inside = (offset >= 0) & (offset < counts[i])
            here = i * patch_len + ranking[i, jnp.clip(offset, 0, patch_len - 1)]
            source = jnp.where(inside, here, source)
            start = start + counts[i]
        rows[pl.ds(j, 1), :] = pt[pl.ds(source, 1), :]
        return carry

    patch_load.wait()
    lax.fori_loop(0, R, take, 0, unroll=8)

    pre[...] = jnp.broadcast_to(ebias[...].astype(jnp.float32)[None, :], pre.shape)
    x = rows[...]
    s1 = jnp.sum(x, axis=1, keepdims=True)
    s2 = jnp.sum(x * x, axis=1, keepdims=True)
    place = lax.broadcasted_iota(jnp.int32, (R, 2 * R), 1) - lax.broadcasted_iota(jnp.int32, (R, 2 * R), 0)
    packed = jnp.sum(jnp.where(place == 0, s1, jnp.where(place == R, s2, 0.0)), axis=0, keepdims=True)
    st[t] = jnp.broadcast_to(packed, st.shape[1:])
    pl.semaphore_wait(barrier, Z + T - 2)

    def stat_copy(k):
        return copy(st.at[t], st.at[t], st_s, st_r, "tensor", lax.rem(t + k, T))

    for k in range(1, T):
        stat_copy(k).start()
    loop(0, C // G * T, lambda n: expand_load(n).start())
    loop(0, T, lambda i: reduce_load(i).start())
    others = st.at[0 : T - 1]
    stats = copy(others, others, st_s, st_r, "tensor", t_part)
    stats.wait_recv()
    both = st[0, 0:1, :]
    for k in range(1, T):
        both = both + st[k, 0:1, :]
    total = [
        jnp.sum(jnp.where(place == k * R, both, 0.0), axis=1, keepdims=True) for k in range(2)
    ]
    gain_row = gain[...][None, :]
    mean = total[0] / D
    var = total[1] / D - mean * mean
    scale = lax.rsqrt(var + 1e-06)
    mine = pl.ds(pl.multiple_of(z * R, R), R)
    for p in range(C):
        cols = slice(p * dlc, (p + 1) * dlc)
        xg[t, p, mine, :] = ((rows[:, cols] - mean) * scale * gain_row[:, cols]).astype(jnp.bfloat16)

    def rows_of(tt, p, zb):
        return xg.at[tt, p, pl.ds(pl.multiple_of(zb * R, R), R), :]

    def inside(i):
        return (i >= 0) & (i < Z)

    def z_copy(way, d, p):
        step = 1 - 2 * way
        ref = rows_of(t, p, z - step * (d - 1))
        return copy(ref, ref, za_s.at[way, d - 1], za_r.at[way, d - 1, p], "dp", z + step)

    def z_sends(way, d):
        step = 1 - 2 * way
        return inside(z - step * (d - 1)) & inside(z + step)

    def z_wait(way, d, p):
        ref = rows_of(t, p, 0)
        copy(ref, ref, za_s.at[way, d - 1], za_r.at[way, d - 1, p], "dp", z_next).wait_recv()

    def y_copy(u, zb, p):
        ref = rows_of(t_of(u - 1, c), p, zb)
        return copy(ref, ref, ya_s.at[u - 1], ya_r.at[u - 1, p // G], "tensor", t_next)

    def c_copy(u, p):
        ref = xg.at[t_of(u, c), p]
        return copy(ref, ref, ca_s.at[u], ca_r.at[u, p // G], "tensor", t_part)

    def z_send(d, p):
        for way in range(2):
            @pl.when(z_sends(way, d))
            def _():
                z_copy(way, d, p).start()

    def z_arrive(d, p):
        for way in range(2):
            step = 1 - 2 * way
            zb = z - step * d

            @pl.when(inside(zb))
            def _():
                z_wait(way, d, p)
                if d < Z - 1:
                    @pl.when(inside(z + step))
                    def _():
                        z_copy(way, d + 1, p).start()

                if Y > 1:
                    y_copy(1, zb, p).start()

    def expand(n):
        q = n // T
        k = n - q * T
        u = k // 2
        tt = t_of(u, c + (k - 2 * u) * (1 - 2 * c))

        @pl.when(k == 0)
        def _():
            ref = wv.at[pl.ds(q * T, T)]
            pltpu.make_async_copy(ref, ref, wsem.at[q]).wait()

        acc = pre[...]
        for g in range(G):
            acc += lax.dot_general(
                xg[tt, q * G + g], wv[n, :, g * dlc : (g + 1) * dlc], (((1,), (1,)), ((), ())),
                preferred_element_type=jnp.float32,
            )
        pre[...] = acc

    def own_sends(p):
        z_send(1, p)
        if Y > 1:
            y_copy(1, z, p).start()

    loop(0, C, own_sends)
    for d in range(1, Z - 1):
        loop(0, C, functools.partial(z_arrive, d))

    Q = C // G
    dots = [(r, q) for r in range(2) for q in range(Q)]
    for u in range(1, Y):
        for q in range(Q + 1):
            dots += [(2 * u, q)] * (q < Q) + [(2 * u + 1, q - 1)] * (q > 0)

    def look(table, i):
        found = table[0]
        for j in range(1, len(table)):
            found = jnp.where(i == j, table[j], found)
        return found

    def step(i):
        r = look([dot[0] for dot in dots], i)
        q = look([dot[1] for dot in dots], i)
        u = r // 2
        odd = r - 2 * u

        @pl.when(r == 0)
        def _():
            for g in range(G):
                if Z > 1:
                    z_arrive(Z - 1, q * G + g)
                c_copy(0, q * G + g).start()

        @pl.when(odd == 1)
        def _():
            ref = xg.at[0, pl.ds(q * G, G)]
            copy(ref, ref, ca_s.at[u], ca_r.at[u, q], "tensor", t_part).wait_recv()

        @pl.when((odd == 0) & (r > 0))
        def _():
            ref = xg.at[0, pl.ds(q * G, G)]
            copy(ref, ref, ya_s.at[u - 1], ya_r.at[u - 1, q], "tensor", t_next).wait_recv()
            for g in range(G):
                p = q * G + g
                if Y > 2:
                    @pl.when(u < Y - 1)
                    def _():
                        for zb in range(Z):
                            y_copy(u + 1, zb, p).start()
                c_copy(u, p).start()

        expand(q * T + r)

    loop(0, T * Q, step)

    def activate(n):
        units = slice(None) if nt == hl else pl.ds(pl.multiple_of(n * nt, nt), nt)
        hid[:, units] = jax.nn.gelu(pre[:, units], approximate=True).astype(jnp.bfloat16)

    if nt == hl:
        activate(0)
    else:
        loop(0, hl // nt, activate)

    def cr_copy(i):
        return copy(cs.at[i], cr.at[i], cr_s, cr_r.at[i], "tensor", t_part)

    def half_of(h):
        return slice(h * M // 2, (h + 1) * M // 2)

    def yr_copy(u, p, h):
        half = half_of(h)
        return copy(
            ys.at[u - 1, p, half, :], yr.at[u - 1, p, half, :],
            yr_s.at[u - 1], yr_r.at[u - 1, p, h], "tensor", t_next,
        )

    def yf_copy(b):
        return copy(yf.at[0, b], yf.at[1, b], yf_s.at[b], yf_r.at[b], "tensor", t_next)

    def rows_at(i):
        return pl.ds(pl.multiple_of(i * R, R), R)

    def direct(slot):
        return (slot >= NA - LAST) & (slot < NA)

    def zr_copy(slot, way, k, whole=False):
        step = 1 - 2 * way
        src = zs.at[slot, rows_at(z + step * k), :]
        if k <= 2 or whole:
            dst, sem, there = zr.at[slot, way, k - 1], zr_r.at[slot, way], z + step * k
        else:
            dst, sem, there = zl.at[slot, way, k - 3], zl_r.at[slot, way, k - 3], z + step
        return copy(src, dst, zr_s.at[way, k - 1], sem, "dp", there)

    def zl_wait(slot, way, k):
        src = zs.at[slot, rows_at(0), :]
        copy(src, zl.at[slot, way, k - 2], zr_s.at[way, k - 1], zl_r.at[slot, way, k - 2], "dp", z_next).wait_recv()

    def z_scatter(slot, h):
        for k in range(Z - 1, 0, -1):
            for way in range(2):
                step = 1 - 2 * way
                to = (z + step * k >= h * Z // 2) & (z + step * k < (h + 1) * Z // 2)
                if 2 <= k < Z - 1:
                    to = to & (direct(slot) | jnp.logical_not(inside(z - step)))
                if k > 2:
                    @pl.when(to & direct(slot))
                    def _():
                        zr_copy(slot, way, k, True).start()

                    to = to & jnp.logical_not(direct(slot))

                @pl.when(to)
                def _():
                    zr_copy(slot, way, k).start()

    def z_relay(slot, at):
        for k in range(Z - 2, 1, -1):
            for way in range(2):
                step = 1 - 2 * way

                @pl.when(inside(z - step) & inside(z + step * k))
                def _():
                    zl_wait(slot, way, k)
                    part = rows_at(z + step * k)
                    v = own[at, part, :] + zl[slot, way, k - 2].astype(jnp.float32)
                    zs[slot, part, :] = v.astype(jnp.bfloat16)
                    zr_copy(slot, way, k).start()

    def z_total(slot, at):
        for way in range(2):
            count = z if way == 0 else Z - 1 - z
            count = jnp.where(direct(slot), count, jnp.minimum(count, 2))
            for k in range(1, Z):
                @pl.when(count == k)
                def _():
                    ref = zr.at[slot, way, 0:k]
                    copy(ref, ref, zr_s.at[way, 0], zr_r.at[slot, way], "dp", z_next).wait_recv()

            for k in range(1, Z):
                @pl.when(count >= k)
                def _():
                    own[at, mine, :] += zr[slot, way, k - 1].astype(jnp.float32)

    def columns(p):
        return slice(None) if C2 == 1 else pl.ds(pl.multiple_of(p * w2, w2), w2)

    NA = C2 - NB
    first = [(0, p) for p in range(NA)]
    if NB:
        rest = [(u, NA + b) for u in range(Y) for b in range(NB)] + [(1, p) for p in range(NA)]
    else:
        rest = [(u, p) for u in range(1, Y) for p in range(NA)]
    order = []
    if NB:
        while first or rest:
            order += first[:1] + rest[:1]
            first, rest = first[1:], rest[1:]
    else:
        order = first + rest
    steps = len(order)

    def chunk(i):
        i = jnp.clip(i, 0, steps - 1)
        return look([o[0] for o in order], i), look([o[1] for o in order], i)

    def slot_of(u, p):
        return jnp.where(u == Y - 1, p, p + NB)

    def scattered(u, p):
        return (u == Y - 1) | (p >= NA)

    def produce(i):
        u, p = chunk(i)
        at = u * C2 + p

        def one(j):
            n = 2 * u + 1 - j
            to = jnp.where(j == 0, Y * C2, at)
            own[to] = jnp.dot(hid[...], rv[n, :, columns(p)], preferred_element_type=jnp.float32)

            @pl.when(j == 0)
            def _():
                cs[at] = own[Y * C2].astype(jnp.bfloat16)
                cr_copy(at).start()

        loop(0, 2, one)

    def combine(i):
        u, p = chunk(i)
        at = u * C2 + p
        cr_copy(at).wait_recv()
        ringed = (u > 0) & (p < NA)
        for h in range(2):
            half = half_of(h)
            own[at, half, :] += cr[at, half, :].astype(jnp.float32)

            @pl.when(ringed)
            def _():
                yr_copy(u, p, h).wait_recv()
                own[at, half, :] += yr[u - 1, p, half, :].astype(jnp.float32)

            @pl.when(scattered(u, p))
            def _():
                zs[slot_of(u, p), half, :] = own[at, half, :].astype(jnp.bfloat16)
                z_scatter(slot_of(u, p), h)

            @pl.when(jnp.logical_not(scattered(u, p)))
            def _():
                ys[u, p, half, :] = own[at, half, :].astype(jnp.bfloat16)
                yr_copy(u + 1, p, h).start()

    def relay(i):
        u, p = chunk(i)

        @pl.when(scattered(u, p) & jnp.logical_not(direct(slot_of(u, p))))
        def _():
            z_relay(slot_of(u, p), u * C2 + p)

    def cross(b):
        at = NA + b
        z_total(C2 + b, at)
        yf[0, b] = own[at, mine, :].astype(jnp.bfloat16)
        yf_copy(b).start()

    def reduce(i):
        @pl.when(i == 0)
        def _():
            pltpu.make_async_copy(rv, rv, rsem).wait()

        @pl.when(i < steps)
        def _():
            produce(i)

        if Z > 3:
            @pl.when(i > 2)
            def _():
                relay(i - 3)

        @pl.when((i > 0) & (i <= steps))
        def _():
            combine(i - 1)

        for b in range(NB):
            @pl.when(i == steps)
            def _():
                cross(b)

    loop(0, steps + 3, reduce)

    last[...] = rbias[...][None, :]

    def drain():
        stats.wait_send()
        for way in range(2):
            step = 1 - 2 * way
            for d in range(1, Z):
                @pl.when(z_sends(way, d))
                def _():
                    ref = xg.at[0, :, rows_at(0), :]
                    copy(ref, ref, za_s.at[way, d - 1], za_r.at[way, 0, 0], "dp", z_next).wait_send()

                @pl.when(inside(z + step * d))
                def _():
                    ref = zs.at[:, rows_at(0), :]
                    copy(ref, ref, zr_s.at[way, d - 1], zr_r.at[0, way], "dp", z_next).wait_send()

        for u in range(Y):
            copy(xg.at[0], xg.at[0], ca_s.at[u], ca_r.at[u, 0], "tensor", t_part).wait_send()
        copy(cs, cr, cr_s, cr_r.at[0], "tensor", t_part).wait_send()
        for u in range(1, Y):
            ref = ys.at[u - 1, 0:NA]
            copy(xg.at[0], xg.at[0], ya_s.at[u - 1], ya_r.at[0, 0], "tensor", t_next).wait_send()
            copy(ref, ref, yr_s.at[u - 1], yr_r.at[0, 0, 0], "tensor", t_next).wait_send()
        for b in range(NB):
            yf_copy(b).wait_send()

    def finish(i):
        @pl.when(i == C2 - 1)
        def _():
            drain()

        p = lax.rem(i + NA, C2)
        at = (Y - 1) * C2 + p
        z_total(p, at)
        for b in range(NB):
            @pl.when(p == NA + b)
            def _():
                yf_copy(b).wait_recv()
                own[at, mine, :] += yf[1, b].astype(jnp.float32)

        cols = columns(p)
        add = own[at, mine, :] + last[:, cols]
        top = add.astype(jnp.bfloat16)
        rest = add - top.astype(jnp.float32)
        middle = rest.astype(jnp.bfloat16)
        low = (rest - middle.astype(jnp.float32)).astype(jnp.bfloat16)
        spread = jnp.dot(pick[...], low, preferred_element_type=jnp.float32)
        spread = spread + jnp.dot(pick[...], middle, preferred_element_type=jnp.float32)
        spread = spread + jnp.dot(pick[...], top, preferred_element_type=jnp.float32)
        pt[:, cols] = pt[:, cols] + spread

    loop(0, C2, finish)


def body(
    Z, T, patches, counts, ranking, norm_gain, expand_weight, expand_bias, reduce_weight, reduce_bias
):
    images, patch_len, dl = patches.shape
    hl, D = expand_weight.shape
    flat = patches.reshape(images * patch_len, dl)
    R, M, Y = CAP, Z * CAP, T // 2
    C = dl // 256 if dl % 256 == 0 else 1
    w2 = 256 if dl % 256 == 0 else dl
    C2 = dl // w2
    G = 2 if C % 2 == 0 else 1
    NB = 1 if Y == 2 and C2 > 4 else 0
    slots = C2 + NB
    dlc = dl // C
    vmem = pl.BlockSpec(memory_space=pltpu.VMEM)
    hbm = pl.BlockSpec(memory_space=pl.ANY)
    bf16, f32 = jnp.bfloat16, jnp.float32
    dma = pltpu.SemaphoreType.DMA
    N = images * patch_len
    smem = pl.BlockSpec(memory_space=pltpu.SMEM)
    result = pl.pallas_call(
        functools.partial(block_kernel, Z, T, C, G, C2, NB),
        out_shape=pltpu.VMEM((N, dl), f32),
        in_specs=[smem] * 2 + [vmem] * 4 + [hbm] * 3,
        out_specs=vmem,
        scratch_shapes=[
            pltpu.VMEM((R, dl), f32),
            pltpu.VMEM((N, R), bf16),
            pltpu.VMEM((T, C, M, dlc), bf16),
            pltpu.VMEM((T * C // G, hl, G * dlc), bf16),
            pltpu.VMEM((T, hl, dl), bf16),
            pltpu.VMEM((M, hl), f32),
            pltpu.VMEM((M, hl), bf16),
            pltpu.VMEM((1, dl), f32),
            pltpu.VMEM((T, 8, 2 * R), f32),
            pltpu.VMEM((Y * C2, M, w2), bf16),
            pltpu.VMEM((Y * C2, M, w2), bf16),
            pltpu.VMEM((Y * C2 + 1, M, w2), f32),
            pltpu.VMEM((Y - 1, C2, M, w2), bf16),
            pltpu.VMEM((Y - 1, C2, M, w2), bf16),
            pltpu.VMEM((slots, M, w2), bf16),
            pltpu.VMEM((slots, 2, Z - 1, R, w2), bf16),
            pltpu.VMEM((slots, 2, max(Z - 3, 1), R, w2), bf16),
            pltpu.VMEM((2, max(NB, 1), R, w2), bf16),
            dma, dma((C // G,)), dma, dma, dma,
            dma((2, Z - 1)), dma((2, Z - 1, C)),
            dma((Y - 1,)), dma((Y - 1, C // G)),
            dma((Y,)), dma((Y, C // G)),
            dma, dma((Y * C2,)),
            dma((Y - 1,)), dma((Y - 1, C2 - NB, 2)),
            dma((2, Z - 1)), dma((slots, 2)), dma((slots, 2, max(Z - 3, 1))),
            dma((max(NB, 1),)), dma((max(NB, 1),)),
        ],
        compiler_params=pltpu.CompilerParams(
            collective_id=0, has_side_effects=True, vmem_limit_bytes=63700000
        ),
        name="feed_forward",
    )(
        counts, ranking, ranking, norm_gain, expand_bias, reduce_bias, flat, expand_weight, reduce_weight,
    )
    return result.reshape(images, patch_len, dl)


def solution(mesh):
    placed = (
        P(("groups", "dp"), None, "tensor"),
        P(("groups", "dp")),
        P(("groups", "dp"), None),
        P("tensor"),
        P(("dp", "tensor"), None),
        P(("dp", "tensor")),
        P(("dp", "tensor"), None),
        P("tensor"),
    )
    return jax.shard_map(
        functools.partial(body, mesh.shape["dp"], mesh.shape["tensor"]),
        mesh=mesh,
        in_specs=placed,
        out_specs=P(("groups", "dp"), None, "tensor"),
        check_vma=False,
    )
```

```python
import functools

import jax
import jax.numpy as jnp
from jax import lax
from jax.experimental import pallas as pl
from jax.experimental.pallas import tpu as pltpu
from jax.sharding import PartitionSpec as P

CAP = 64
LAST = 1
MESH = pl.DeviceIdType.MESH


def block_kernel(
    Z, T, C, G, C2, NB, counts, ranking, ranking_v, gain, ebias, rbias, flat, e_hbm, r_hbm, pt,
    rows, pick,    xg, wv, rv, pre, hid, last, st, cs, cr, own, ys, yr, zs, zr, zl, yf,
    psem, wsem, rsem, st_s, st_r, za_s, za_r, ya_s, ya_r, ca_s, ca_r,
    cr_s, cr_r, yr_s, yr_r, zr_s, zr_r, zl_r, yf_s, yf_r,
):
    Y = T // 2
    R, dl = rows.shape
    images, patch_len = ranking.shape
    N = images * patch_len
    hl, D = e_hbm.shape
    M, dlc, w2 = Z * R, dl // C, dl // C2
    nt = 256 if hl % 256 == 0 else hl
    z = lax.axis_index("dp")
    t = lax.axis_index("tensor")
    y, c = t // 2, t % 2
    z_next = lax.rem(z + 1, Z)
    t_next = lax.rem(y + 1, Y) * 2 + c
    t_part = y * 2 + 1 - c

    barrier = pltpu.get_barrier_semaphore()
    for k in range(1, Z):
        pl.semaphore_signal(barrier, inc=1, device_id={"dp": lax.rem(z + k, Z)}, device_id_type=MESH)
    for k in range(1, T):
        pl.semaphore_signal(barrier, inc=1, device_id={"tensor": lax.rem(t + k, T)}, device_id_type=MESH)

    def copy(src, dst, ss, rs, axis, index):
        return pltpu.make_async_remote_copy(
            src_ref=src, dst_ref=dst, send_sem=ss, recv_sem=rs,
            device_id={axis: index}, device_id_type=MESH,
        )

    def t_of(u, core):
        return lax.rem(y - u + Y, Y) * 2 + core

    def t_red(u, core):
        return lax.rem(y - 1 - u + 2 * Y, Y) * 2 + core

    def loop(low, high, body):
        lax.fori_loop(low, high, lambda p, a: (body(p), a)[1], 0)

    def expand_load(n):
        q = n // T
        k = n - q * T
        u = k // 2
        core = c + (k - 2 * u) * (1 - 2 * c)
        lanes = pl.ds(pl.multiple_of(t_of(u, core) * dl + q * G * dlc, 128), G * dlc)
        return pltpu.make_async_copy(e_hbm.at[:, lanes], wv.at[n], wsem.at[q])

    def reduce_load(i):
        u = i // 2
        block = t_red(u, c + (i - 2 * u) * (1 - 2 * c))
        lanes = pl.ds(pl.multiple_of(block * dl, 128), dl)
        return pltpu.make_async_copy(r_hbm.at[:, lanes], rv.at[i], rsem)

    patch_load = pltpu.make_async_copy(flat, pt, psem)
    patch_load.start()

    lane_w = images * R
    which = lax.broadcasted_iota(jnp.int32, (1, lane_w), 1)
    rank, owner = jnp.full((1, lane_w), -1, jnp.int32), jnp.full((1, lane_w), -1, jnp.int32)
    start = 0
    for i in range(images):
        k = which - i * R
        live = (k >= 0) & (k < counts[i])
        owner = jnp.where(live, start + k, owner)
        start = start + counts[i]
        known = jnp.concatenate([ranking_v[i : i + 1, :R]] * images, axis=1)
        rank = jnp.where(live, i * patch_len + known, rank)
    chosen = jnp.where(lax.broadcasted_iota(jnp.int32, (N, lane_w), 0) == rank, 1.0, 0.0)
    slot = jnp.where(lax.broadcasted_iota(jnp.int32, (R, lane_w), 0) == owner, 1.0, 0.0)
    pick[...] = lax.dot_general(
        chosen.astype(jnp.bfloat16), slot.astype(jnp.bfloat16), (((1,), (1,)), ((), ())),
        preferred_element_type=jnp.float32,
    ).astype(jnp.bfloat16)

    def source(j):
        start, found = 0, 0
        for i in range(images):
            offset = j - start
            inside_it = (offset >= 0) & (offset < counts[i])
            here = i * patch_len + ranking[i, jnp.clip(offset, 0, patch_len - 1)]
            found = jnp.where(inside_it, here, found)
            start = start + counts[i]
        return found

    def take(g):
        line = lax.broadcasted_iota(jnp.int32, (8, dl), 0)
        eight = jnp.zeros((8, dl), jnp.float32)
        for r in range(8):
            eight = jnp.where(line == r, pt[pl.ds(source(g * 8 + r), 1), :], eight)
        rows[pl.ds(pl.multiple_of(g * 8, 8), 8), :] = eight

    patch_load.wait()
    loop(0, R // 8, take)

    pre[...] = jnp.broadcast_to(ebias[...].astype(jnp.float32)[None, :], pre.shape)
    x = rows[...]
    s1 = jnp.sum(x, axis=1, keepdims=True)
    s2 = jnp.sum(x * x, axis=1, keepdims=True)
    place = lax.broadcasted_iota(jnp.int32, (R, 2 * R), 1) - lax.broadcasted_iota(jnp.int32, (R, 2 * R), 0)
    packed = jnp.sum(jnp.where(place == 0, s1, jnp.where(place == R, s2, 0.0)), axis=0, keepdims=True)
    st[t] = jnp.broadcast_to(packed, st.shape[1:])
    pl.semaphore_wait(barrier, Z + T - 2)

    def stat_copy(k):
        return copy(st.at[t], st.at[t], st_s, st_r, "tensor", lax.rem(t + k, T))

    for k in range(1, T):
        stat_copy(k).start()
    loop(0, C // G * T, lambda n: expand_load(n).start())
    loop(0, T, lambda i: reduce_load(i).start())
    others = st.at[0 : T - 1]
    stats = copy(others, others, st_s, st_r, "tensor", t_part)
    stats.wait_recv()
    both = st[0, 0:1, :]
    for k in range(1, T):
        both = both + st[k, 0:1, :]
    total = [
        jnp.sum(jnp.where(place == k * R, both, 0.0), axis=1, keepdims=True) for k in range(2)
    ]
    gain_row = gain[...][None, :]
    mean = total[0] / D
    var = total[1] / D - mean * mean
    scale = lax.rsqrt(var + 1e-06)
    mine = pl.ds(pl.multiple_of(z * R, R), R)
    for p in range(C):
        cols = slice(p * dlc, (p + 1) * dlc)
        xg[t, p, mine, :] = ((rows[:, cols] - mean) * scale * gain_row[:, cols]).astype(jnp.bfloat16)

    def rows_of(tt, p, zb):
        return xg.at[tt, p, pl.ds(pl.multiple_of(zb * R, R), R), :]

    def inside(i):
        return (i >= 0) & (i < Z)

    def z_copy(way, d, p):
        step = 1 - 2 * way
        ref = rows_of(t, p, z - step * (d - 1))
        return copy(ref, ref, za_s.at[way, d - 1], za_r.at[way, d - 1, p], "dp", z + step)

    def z_sends(way, d):
        step = 1 - 2 * way
        return inside(z - step * (d - 1)) & inside(z + step)

    def z_wait(way, d, p):
        ref = rows_of(t, p, 0)
        copy(ref, ref, za_s.at[way, d - 1], za_r.at[way, d - 1, p], "dp", z_next).wait_recv()

    def y_copy(u, zb, p):
        ref = rows_of(t_of(u - 1, c), p, zb)
        return copy(ref, ref, ya_s.at[u - 1], ya_r.at[u - 1, p // G], "tensor", t_next)

    def c_copy(u, p):
        ref = xg.at[t_of(u, c), p]
        return copy(ref, ref, ca_s.at[u], ca_r.at[u, p // G], "tensor", t_part)

    def z_send(d, p):
        for way in range(2):
            @pl.when(z_sends(way, d))
            def _():
                z_copy(way, d, p).start()

    def z_arrive(d, p):
        for way in range(2):
            step = 1 - 2 * way
            zb = z - step * d

            @pl.when(inside(zb))
            def _():
                z_wait(way, d, p)
                if d < Z - 1:
                    @pl.when(inside(z + step))
                    def _():
                        z_copy(way, d + 1, p).start()

                if Y > 1:
                    y_copy(1, zb, p).start()

    def expand(n):
        q = n // T
        k = n - q * T
        u = k // 2
        tt = t_of(u, c + (k - 2 * u) * (1 - 2 * c))

        @pl.when(k == 0)
        def _():
            ref = wv.at[pl.ds(q * T, T)]
            pltpu.make_async_copy(ref, ref, wsem.at[q]).wait()

        acc = pre[...]
        for g in range(G):
            acc += lax.dot_general(
                xg[tt, q * G + g], wv[n, :, g * dlc : (g + 1) * dlc], (((1,), (1,)), ((), ())),
                preferred_element_type=jnp.float32,
            )
        pre[...] = acc

    def own_sends(p):
        z_send(1, p)
        if Y > 1:
            y_copy(1, z, p).start()

    loop(0, C, own_sends)
    for d in range(1, Z - 1):
        loop(0, C, functools.partial(z_arrive, d))

    Q = C // G
    dots = [(r, q) for r in range(2) for q in range(Q)]
    for u in range(1, Y):
        for q in range(Q + 1):
            dots += [(2 * u, q)] * (q < Q) + [(2 * u + 1, q - 1)] * (q > 0)

    def look(table, i):
        found = table[0]
        for j in range(1, len(table)):
            found = jnp.where(i == j, table[j], found)
        return found

    def step(i):
        r = look([dot[0] for dot in dots], i)
        q = look([dot[1] for dot in dots], i)
        u = r // 2
        odd = r - 2 * u

        @pl.when(r == 0)
        def _():
            for g in range(G):
                if Z > 1:
                    z_arrive(Z - 1, q * G + g)
                c_copy(0, q * G + g).start()

        @pl.when(odd == 1)
        def _():
            ref = xg.at[0, pl.ds(q * G, G)]
            copy(ref, ref, ca_s.at[u], ca_r.at[u, q], "tensor", t_part).wait_recv()

        @pl.when((odd == 0) & (r > 0))
        def _():
            ref = xg.at[0, pl.ds(q * G, G)]
            copy(ref, ref, ya_s.at[u - 1], ya_r.at[u - 1, q], "tensor", t_next).wait_recv()
            for g in range(G):
                p = q * G + g
                if Y > 2:
                    @pl.when(u < Y - 1)
                    def _():
                        for zb in range(Z):
                            y_copy(u + 1, zb, p).start()
                c_copy(u, p).start()

        expand(q * T + r)

    loop(0, T * Q, step)

    def activate(n):
        units = slice(None) if nt == hl else pl.ds(pl.multiple_of(n * nt, nt), nt)
        hid[:, units] = jax.nn.gelu(pre[:, units], approximate=True).astype(jnp.bfloat16)

    if nt == hl:
        activate(0)
    else:
        loop(0, hl // nt, activate)

    def cr_copy(i):
        return copy(cs.at[i], cr.at[i], cr_s, cr_r.at[i], "tensor", t_part)

    def half_of(h):
        return slice(h * M // 2, (h + 1) * M // 2)

    def yr_copy(u, p, h):
        half = half_of(h)
        return copy(
            ys.at[u - 1, p, half, :], yr.at[u - 1, p, half, :],
            yr_s.at[u - 1], yr_r.at[u - 1, p, h], "tensor", t_next,
        )

    def yf_copy(b):
        return copy(yf.at[0, b], yf.at[1, b], yf_s.at[b], yf_r.at[b], "tensor", t_next)

    def rows_at(i):
        return pl.ds(pl.multiple_of(i * R, R), R)

    def direct(slot):
        return (slot >= NA - LAST) & (slot < NA)

    def zr_copy(slot, way, k, whole=False):
        step = 1 - 2 * way
        src = zs.at[slot, rows_at(z + step * k), :]
        if k <= 2 or whole:
            dst, sem, there = zr.at[slot, way, k - 1], zr_r.at[slot, way], z + step * k
        else:
            dst, sem, there = zl.at[slot, way, k - 3], zl_r.at[slot, way, k - 3], z + step
        return copy(src, dst, zr_s.at[way, k - 1], sem, "dp", there)

    def zl_wait(slot, way, k):
        src = zs.at[slot, rows_at(0), :]
        copy(src, zl.at[slot, way, k - 2], zr_s.at[way, k - 1], zl_r.at[slot, way, k - 2], "dp", z_next).wait_recv()

    def z_scatter(slot, h):
        for k in range(Z - 1, 0, -1):
            for way in range(2):
                step = 1 - 2 * way
                to = (z + step * k >= h * Z // 2) & (z + step * k < (h + 1) * Z // 2)
                if 2 <= k < Z - 1:
                    to = to & (direct(slot) | jnp.logical_not(inside(z - step)))
                if k > 2:
                    @pl.when(to & direct(slot))
                    def _():
                        zr_copy(slot, way, k, True).start()

                    to = to & jnp.logical_not(direct(slot))

                @pl.when(to)
                def _():
                    zr_copy(slot, way, k).start()

    def z_relay(slot, at):
        for k in range(Z - 2, 1, -1):
            for way in range(2):
                step = 1 - 2 * way

                @pl.when(inside(z - step) & inside(z + step * k))
                def _():
                    zl_wait(slot, way, k)
                    part = rows_at(z + step * k)
                    v = own[at, part, :] + zl[slot, way, k - 2].astype(jnp.float32)
                    zs[slot, part, :] = v.astype(jnp.bfloat16)
                    zr_copy(slot, way, k).start()

    def z_total(slot, at):
        for way in range(2):
            count = z if way == 0 else Z - 1 - z
            count = jnp.where(direct(slot), count, jnp.minimum(count, 2))
            for k in range(1, Z):
                @pl.when(count == k)
                def _():
                    ref = zr.at[slot, way, 0:k]
                    copy(ref, ref, zr_s.at[way, 0], zr_r.at[slot, way], "dp", z_next).wait_recv()

            for k in range(1, Z):
                @pl.when(count >= k)
                def _():
                    own[at, mine, :] += zr[slot, way, k - 1].astype(jnp.float32)

    def columns(p):
        return slice(None) if C2 == 1 else pl.ds(pl.multiple_of(p * w2, w2), w2)

    NA = C2 - NB
    first = [(0, p) for p in range(NA)]
    if NB:
        rest = [(u, NA + b) for u in range(Y) for b in range(NB)] + [(1, p) for p in range(NA)]
    else:
        rest = [(u, p) for u in range(1, Y) for p in range(NA)]
    order = []
    if NB:
        while first or rest:
            order += first[:1] + rest[:1]
            first, rest = first[1:], rest[1:]
    else:
        order = first + rest
    steps = len(order)

    def chunk(i):
        i = jnp.clip(i, 0, steps - 1)
        return look([o[0] for o in order], i), look([o[1] for o in order], i)

    def slot_of(u, p):
        return jnp.where(u == Y - 1, p, p + NB)

    def scattered(u, p):
        return (u == Y - 1) | (p >= NA)

    def produce(i):
        u, p = chunk(i)
        at = u * C2 + p

        def one(j):
            n = 2 * u + 1 - j
            to = jnp.where(j == 0, Y * C2, at)
            own[to] = jnp.dot(hid[...], rv[n, :, columns(p)], preferred_element_type=jnp.float32)

            @pl.when(j == 0)
            def _():
                cs[at] = own[Y * C2].astype(jnp.bfloat16)
                cr_copy(at).start()

        loop(0, 2, one)

    def combine(i):
        u, p = chunk(i)
        at = u * C2 + p
        cr_copy(at).wait_recv()
        ringed = (u > 0) & (p < NA)
        for h in range(2):
            half = half_of(h)
            own[at, half, :] += cr[at, half, :].astype(jnp.float32)

            @pl.when(ringed)
            def _():
                yr_copy(u, p, h).wait_recv()
                own[at, half, :] += yr[u - 1, p, half, :].astype(jnp.float32)

            @pl.when(scattered(u, p))
            def _():
                zs[slot_of(u, p), half, :] = own[at, half, :].astype(jnp.bfloat16)
                z_scatter(slot_of(u, p), h)

            @pl.when(jnp.logical_not(scattered(u, p)))
            def _():
                ys[u, p, half, :] = own[at, half, :].astype(jnp.bfloat16)
                yr_copy(u + 1, p, h).start()

    def relay(i):
        u, p = chunk(i)

        @pl.when(scattered(u, p) & jnp.logical_not(direct(slot_of(u, p))))
        def _():
            z_relay(slot_of(u, p), u * C2 + p)

    def cross(b):
        at = NA + b
        z_total(C2 + b, at)
        yf[0, b] = own[at, mine, :].astype(jnp.bfloat16)
        yf_copy(b).start()

    def reduce(i):
        @pl.when(i == 0)
        def _():
            pltpu.make_async_copy(rv, rv, rsem).wait()

        @pl.when(i < steps)
        def _():
            produce(i)

        if Z > 3:
            @pl.when(i > 2)
            def _():
                relay(i - 3)

        @pl.when((i > 0) & (i <= steps))
        def _():
            combine(i - 1)

        for b in range(NB):
            @pl.when(i == steps)
            def _():
                cross(b)

    loop(0, steps + 3, reduce)

    last[...] = rbias[...][None, :]

    def drain():
        stats.wait_send()
        for way in range(2):
            step = 1 - 2 * way
            for d in range(1, Z):
                @pl.when(z_sends(way, d))
                def _():
                    ref = xg.at[0, :, rows_at(0), :]
                    copy(ref, ref, za_s.at[way, d - 1], za_r.at[way, 0, 0], "dp", z_next).wait_send()

                @pl.when(inside(z + step * d))
                def _():
                    ref = zs.at[:, rows_at(0), :]
                    copy(ref, ref, zr_s.at[way, d - 1], zr_r.at[0, way], "dp", z_next).wait_send()

        for u in range(Y):
            copy(xg.at[0], xg.at[0], ca_s.at[u], ca_r.at[u, 0], "tensor", t_part).wait_send()
        copy(cs, cr, cr_s, cr_r.at[0], "tensor", t_part).wait_send()
        for u in range(1, Y):
            ref = ys.at[u - 1, 0:NA]
            copy(xg.at[0], xg.at[0], ya_s.at[u - 1], ya_r.at[0, 0], "tensor", t_next).wait_send()
            copy(ref, ref, yr_s.at[u - 1], yr_r.at[0, 0, 0], "tensor", t_next).wait_send()
        for b in range(NB):
            yf_copy(b).wait_send()

    def finish(i):
        @pl.when(i == C2 - 1)
        def _():
            drain()

        p = lax.rem(i + NA, C2)
        at = (Y - 1) * C2 + p
        z_total(p, at)
        for b in range(NB):
            @pl.when(p == NA + b)
            def _():
                yf_copy(b).wait_recv()
                own[at, mine, :] += yf[1, b].astype(jnp.float32)

        cols = columns(p)
        add = own[at, mine, :] + last[:, cols]
        top = add.astype(jnp.bfloat16)
        rest = add - top.astype(jnp.float32)
        middle = rest.astype(jnp.bfloat16)
        low = (rest - middle.astype(jnp.float32)).astype(jnp.bfloat16)
        spread = jnp.dot(pick[...], low, preferred_element_type=jnp.float32)
        spread = spread + jnp.dot(pick[...], middle, preferred_element_type=jnp.float32)
        spread = spread + jnp.dot(pick[...], top, preferred_element_type=jnp.float32)
        pt[:, cols] = pt[:, cols] + spread

    loop(0, C2, finish)


def body(
    Z, T, patches, counts, ranking, norm_gain, expand_weight, expand_bias, reduce_weight, reduce_bias
):
    images, patch_len, dl = patches.shape
    hl, D = expand_weight.shape
    flat = patches.reshape(images * patch_len, dl)
    R, M, Y = CAP, Z * CAP, T // 2
    C = dl // 256 if dl % 256 == 0 else 1
    w2 = 256 if dl % 256 == 0 else dl
    C2 = dl // w2
    G = 2 if C % 2 == 0 else 1
    NB = 1 if Y == 2 and C2 > 4 else 0
    slots = C2 + NB
    dlc = dl // C
    vmem = pl.BlockSpec(memory_space=pltpu.VMEM)
    hbm = pl.BlockSpec(memory_space=pl.ANY)
    bf16, f32 = jnp.bfloat16, jnp.float32
    dma = pltpu.SemaphoreType.DMA
    N = images * patch_len
    smem = pl.BlockSpec(memory_space=pltpu.SMEM)
    result = pl.pallas_call(
        functools.partial(block_kernel, Z, T, C, G, C2, NB),
        out_shape=pltpu.VMEM((N, dl), f32),
        in_specs=[smem] * 2 + [vmem] * 4 + [hbm] * 3,
        out_specs=vmem,
        scratch_shapes=[
            pltpu.VMEM((R, dl), f32),
            pltpu.VMEM((N, R), bf16),
            pltpu.VMEM((T, C, M, dlc), bf16),
            pltpu.VMEM((T * C // G, hl, G * dlc), bf16),
            pltpu.VMEM((T, hl, dl), bf16),
            pltpu.VMEM((M, hl), f32),
            pltpu.VMEM((M, hl), bf16),
            pltpu.VMEM((1, dl), f32),
            pltpu.VMEM((T, 8, 2 * R), f32),
            pltpu.VMEM((Y * C2, M, w2), bf16),
            pltpu.VMEM((Y * C2, M, w2), bf16),
            pltpu.VMEM((Y * C2 + 1, M, w2), f32),
            pltpu.VMEM((Y - 1, C2, M, w2), bf16),
            pltpu.VMEM((Y - 1, C2, M, w2), bf16),
            pltpu.VMEM((slots, M, w2), bf16),
            pltpu.VMEM((slots, 2, Z - 1, R, w2), bf16),
            pltpu.VMEM((slots, 2, max(Z - 3, 1), R, w2), bf16),
            pltpu.VMEM((2, max(NB, 1), R, w2), bf16),
            dma, dma((C // G,)), dma, dma, dma,
            dma((2, Z - 1)), dma((2, Z - 1, C)),
            dma((Y - 1,)), dma((Y - 1, C // G)),
            dma((Y,)), dma((Y, C // G)),
            dma, dma((Y * C2,)),
            dma((Y - 1,)), dma((Y - 1, C2 - NB, 2)),
            dma((2, Z - 1)), dma((slots, 2)), dma((slots, 2, max(Z - 3, 1))),
            dma((max(NB, 1),)), dma((max(NB, 1),)),
        ],
        compiler_params=pltpu.CompilerParams(
            collective_id=0, has_side_effects=True, vmem_limit_bytes=63700000
        ),
        name="feed_forward",
    )(
        counts, ranking, ranking, norm_gain, expand_bias, reduce_bias, flat, expand_weight, reduce_weight,
    )
    return result.reshape(images, patch_len, dl)


def solution(mesh):
    placed = (
        P(("groups", "dp"), None, "tensor"),
        P(("groups", "dp")),
        P(("groups", "dp"), None),
        P("tensor"),
        P(("dp", "tensor"), None),
        P(("dp", "tensor")),
        P(("dp", "tensor"), None),
        P("tensor"),
    )
    return jax.shard_map(
        functools.partial(body, mesh.shape["dp"], mesh.shape["tensor"]),
        mesh=mesh,
        in_specs=placed,
        out_specs=P(("groups", "dp"), None, "tensor"),
        check_vma=False,
    )
```

```python
import functools

import jax
import jax.numpy as jnp
from jax import lax
from jax.experimental import pallas as pl
from jax.experimental.pallas import tpu as pltpu
from jax.sharding import PartitionSpec as P

CAP = 64
LAST = 1
MESH = pl.DeviceIdType.MESH


def block_kernel(
    Z, T, C, G, C2, NB, counts, ranking, ranking_v, gain, ebias, rbias, flat, e_hbm, r_hbm, pt,
    rows, pick,    xg, wv, rv, pre, hid, last, st, cs, cr, own, ys, yr, zs, zr, zl, yf,
    psem, wsem, rsem, st_s, st_r, za_s, za_r, ya_s, ya_r, ca_s, ca_r,
    cr_s, cr_r, yr_s, yr_r, zr_s, zr_r, zl_r, yf_s, yf_r,
):
    Y = T // 2
    R, dl = rows.shape
    images, patch_len = ranking.shape
    N = images * patch_len
    hl, D = e_hbm.shape
    M, dlc, w2 = Z * R, dl // C, dl // C2
    nt = 256 if hl % 256 == 0 else hl
    z = lax.axis_index("dp")
    t = lax.axis_index("tensor")
    y, c = t // 2, t % 2
    z_next = lax.rem(z + 1, Z)
    t_next = lax.rem(y + 1, Y) * 2 + c
    t_part = y * 2 + 1 - c

    barrier = pltpu.get_barrier_semaphore()
    for k in range(1, Z):
        pl.semaphore_signal(barrier, inc=1, device_id={"dp": lax.rem(z + k, Z)}, device_id_type=MESH)
    for k in range(1, T):
        pl.semaphore_signal(barrier, inc=1, device_id={"tensor": lax.rem(t + k, T)}, device_id_type=MESH)

    def copy(src, dst, ss, rs, axis, index):
        return pltpu.make_async_remote_copy(
            src_ref=src, dst_ref=dst, send_sem=ss, recv_sem=rs,
            device_id={axis: index}, device_id_type=MESH,
        )

    def t_of(u, core):
        return lax.rem(y - u + Y, Y) * 2 + core

    def t_red(u, core):
        return lax.rem(y - 1 - u + 2 * Y, Y) * 2 + core

    def loop(low, high, body):
        lax.fori_loop(low, high, lambda p, a: (body(p), a)[1], 0)

    def expand_load(n):
        q = n // T
        k = n - q * T
        u = k // 2
        core = c + (k - 2 * u) * (1 - 2 * c)
        lanes = pl.ds(pl.multiple_of(t_of(u, core) * dl + q * G * dlc, 128), G * dlc)
        return pltpu.make_async_copy(e_hbm.at[:, lanes], wv.at[n], wsem.at[q])

    def reduce_load(i):
        u = i // 2
        block = t_red(u, c + (i - 2 * u) * (1 - 2 * c))
        lanes = pl.ds(pl.multiple_of(block * dl, 128), dl)
        return pltpu.make_async_copy(r_hbm.at[:, lanes], rv.at[i], rsem)

    patch_load = pltpu.make_async_copy(flat, pt, psem)
    patch_load.start()

    lane_w = images * R
    which = lax.broadcasted_iota(jnp.int32, (1, lane_w), 1)
    rank, owner = jnp.full((1, lane_w), -1, jnp.int32), jnp.full((1, lane_w), -1, jnp.int32)
    start = 0
    for i in range(images):
        k = which - i * R
        live = (k >= 0) & (k < counts[i])
        owner = jnp.where(live, start + k, owner)
        start = start + counts[i]
        known = jnp.concatenate([ranking_v[i : i + 1, :R]] * images, axis=1)
        rank = jnp.where(live, i * patch_len + known, rank)
    chosen = jnp.where(lax.broadcasted_iota(jnp.int32, (N, lane_w), 0) == rank, 1.0, 0.0)
    slot = jnp.where(lax.broadcasted_iota(jnp.int32, (R, lane_w), 0) == owner, 1.0, 0.0)
    pick[...] = lax.dot_general(
        chosen.astype(jnp.bfloat16), slot.astype(jnp.bfloat16), (((1,), (1,)), ((), ())),
        preferred_element_type=jnp.float32,
    ).astype(jnp.bfloat16)

    def source(j):
        start, found = 0, 0
        for i in range(images):
            offset = j - start
            inside_it = (offset >= 0) & (offset < counts[i])
            here = i * patch_len + ranking[i, jnp.clip(offset, 0, patch_len - 1)]
            found = jnp.where(inside_it, here, found)
            start = start + counts[i]
        return found

    def take(g):
        line = lax.broadcasted_iota(jnp.int32, (8, dl), 0)
        eight = jnp.zeros((8, dl), jnp.float32)
        for r in range(8):
            eight = jnp.where(line == r, pt[pl.ds(source(g * 8 + r), 1), :], eight)
        rows[pl.ds(pl.multiple_of(g * 8, 8), 8), :] = eight

    patch_load.wait()
    loop(0, R // 8, take)

    pre[...] = jnp.broadcast_to(ebias[...].astype(jnp.float32)[None, :], pre.shape)
    x = rows[...]
    s1 = jnp.sum(x, axis=1, keepdims=True)
    s2 = jnp.sum(x * x, axis=1, keepdims=True)
    place = lax.broadcasted_iota(jnp.int32, (R, 2 * R), 1) - lax.broadcasted_iota(jnp.int32, (R, 2 * R), 0)
    packed = jnp.sum(jnp.where(place == 0, s1, jnp.where(place == R, s2, 0.0)), axis=0, keepdims=True)
    st[t] = jnp.broadcast_to(packed, st.shape[1:])
    pl.semaphore_wait(barrier, Z + T - 2)

    def stat_copy(k):
        return copy(st.at[t], st.at[t], st_s, st_r, "tensor", lax.rem(t + k, T))

    for k in range(1, T):
        stat_copy(k).start()
    loop(0, C // G * T, lambda n: expand_load(n).start())
    loop(0, T, lambda i: reduce_load(i).start())
    others = st.at[0 : T - 1]
    stats = copy(others, others, st_s, st_r, "tensor", t_part)
    stats.wait_recv()
    both = st[0, 0:1, :]
    for k in range(1, T):
        both = both + st[k, 0:1, :]
    total = [
        jnp.sum(jnp.where(place == k * R, both, 0.0), axis=1, keepdims=True) for k in range(2)
    ]
    gain_row = gain[...][None, :]
    mean = total[0] / D
    var = total[1] / D - mean * mean
    scale = lax.rsqrt(var + 1e-06)
    mine = pl.ds(pl.multiple_of(z * R, R), R)
    for p in range(C):
        cols = slice(p * dlc, (p + 1) * dlc)
        xg[t, p, mine, :] = ((rows[:, cols] - mean) * scale * gain_row[:, cols]).astype(jnp.bfloat16)

    def rows_of(tt, p, zb):
        return xg.at[tt, p, pl.ds(pl.multiple_of(zb * R, R), R), :]

    def inside(i):
        return (i >= 0) & (i < Z)

    def z_copy(way, d, p):
        step = 1 - 2 * way
        ref = rows_of(t, p, z - step * (d - 1))
        return copy(ref, ref, za_s.at[way, d - 1], za_r.at[way, d - 1, p], "dp", z + step)

    def z_sends(way, d):
        step = 1 - 2 * way
        return inside(z - step * (d - 1)) & inside(z + step)

    def z_wait(way, d, p):
        ref = rows_of(t, p, 0)
        copy(ref, ref, za_s.at[way, d - 1], za_r.at[way, d - 1, p], "dp", z_next).wait_recv()

    def y_copy(u, zb, p):
        ref = rows_of(t_of(u - 1, c), p, zb)
        return copy(ref, ref, ya_s.at[u - 1], ya_r.at[u - 1, p // G], "tensor", t_next)

    def c_copy(u, p):
        ref = xg.at[t_of(u, c), p]
        return copy(ref, ref, ca_s.at[u], ca_r.at[u, p // G], "tensor", t_part)

    def z_send(d, p):
        for way in range(2):
            @pl.when(z_sends(way, d))
            def _():
                z_copy(way, d, p).start()

    def z_arrive(d, p):
        for way in range(2):
            step = 1 - 2 * way
            zb = z - step * d

            @pl.when(inside(zb))
            def _():
                z_wait(way, d, p)
                if d < Z - 1:
                    @pl.when(inside(z + step))
                    def _():
                        z_copy(way, d + 1, p).start()

                if Y > 1:
                    y_copy(1, zb, p).start()

    def expand(u, q):
        ref = xg.at[0, pl.ds(q * G, G)]
        copy(ref, ref, ca_s.at[u], ca_r.at[u, q], "tensor", t_part).wait_recv()

        @pl.when(u == 0)
        def _():
            ref = wv.at[pl.ds(q * T, T)]
            pltpu.make_async_copy(ref, ref, wsem.at[q]).wait()

        acc = pre[...]
        for odd in range(2):
            tt = t_of(u, c if odd == 0 else 1 - c)
            for g in range(G):
                acc += lax.dot_general(
                    xg[tt, q * G + g], wv[q * T + 2 * u + odd, :, g * dlc : (g + 1) * dlc],
                    (((1,), (1,)), ((), ())), preferred_element_type=jnp.float32,
                )
        pre[...] = acc

    def own_sends(p):
        z_send(1, p)
        if Y > 1:
            y_copy(1, z, p).start()

    loop(0, C, own_sends)
    for d in range(1, Z - 1):
        loop(0, C, functools.partial(z_arrive, d))

    Q = C // G
    def look(table, i):
        found = table[0]
        for j in range(1, len(table)):
            found = jnp.where(i == j, table[j], found)
        return found

    def arrive(u, q):
        @pl.when(u == 0)
        def _():
            for g in range(G):
                if Z > 1:
                    z_arrive(Z - 1, q * G + g)

        @pl.when(u > 0)
        def _():
            ref = xg.at[0, pl.ds(q * G, G)]
            copy(ref, ref, ya_s.at[u - 1], ya_r.at[u - 1, q], "tensor", t_next).wait_recv()
            if Y > 2:
                @pl.when(u < Y - 1)
                def _():
                    for g in range(G):
                        for zb in range(Z):
                            y_copy(u + 1, zb, q * G + g).start()

        for g in range(G):
            c_copy(u, q * G + g).start()

    def step(i):
        @pl.when(i < Y * Q)
        def _():
            arrive(i // Q, lax.rem(i, Q))

        @pl.when(i > 0)
        def _():
            expand((i - 1) // Q, lax.rem(i - 1, Q))

    loop(0, Y * Q + 1, step)

    def activate(n):
        units = slice(None) if nt == hl else pl.ds(pl.multiple_of(n * nt, nt), nt)
        hid[:, units] = jax.nn.gelu(pre[:, units], approximate=True).astype(jnp.bfloat16)

    if nt == hl:
        activate(0)
    else:
        loop(0, hl // nt, activate)

    def cr_copy(i):
        return copy(cs.at[i], cr.at[i], cr_s, cr_r.at[i], "tensor", t_part)

    parts = [
        look([sorted(range(Z), key=lambda b: -abs(b - a))[h] for a in range(Z)], z) for h in range(Z)
    ]

    def yr_copy(u, p, h):
        part = rows_at(parts[h])
        return copy(
            ys.at[u - 1, p, part, :], yr.at[u - 1, p, part, :],
            yr_s.at[u - 1], yr_r.at[u - 1, p, h], "tensor", t_next,
        )

    def yf_copy(b):
        return copy(yf.at[0, b], yf.at[1, b], yf_s.at[b], yf_r.at[b], "tensor", t_next)

    def rows_at(i):
        return pl.ds(pl.multiple_of(i * R, R), R)

    def direct(slot):
        return (slot >= NA - LAST) & (slot < NA)

    def zr_copy(slot, way, k):
        there = z + (1 - 2 * way) * k
        return copy(
            zs.at[slot, rows_at(there), :], zr.at[slot, way, k - 1],
            zr_s.at[way, k - 1], zr_r.at[slot, way], "dp", there,
        )

    def zl_copy(slot, way, k):
        step = 1 - 2 * way
        return copy(
            zs.at[slot, rows_at(z + step * k), :], zl.at[slot, way, k - 3],
            zr_s.at[way, k - 1], zl_r.at[slot, way, k - 3], "dp", z + step,
        )

    def zl_wait(slot, way, k):
        src = zs.at[slot, rows_at(0), :]
        copy(src, zl.at[slot, way, k - 2], zr_s.at[way, k - 1], zl_r.at[slot, way, k - 2], "dp", z_next).wait_recv()

    def z_scatter(slot, zb):
        way = jnp.where(zb < z, 1, 0)
        k = jnp.where(zb < z, z - zb, zb - z)
        last_one = jnp.logical_not(inside(z - (1 - 2 * way)))

        @pl.when((k > 0) & (direct(slot) | (k == 1) | ((k == 2) & last_one)))
        def _():
            zr_copy(slot, way, k).start()

        if Z > 3:
            @pl.when((k > 2) & last_one & jnp.logical_not(direct(slot)))
            def _():
                zl_copy(slot, way, k).start()

    def z_relay(slot, at):
        for k in range(Z - 2, 1, -1):
            for way in range(2):
                step = 1 - 2 * way

                @pl.when(inside(z - step) & inside(z + step * k))
                def _():
                    zl_wait(slot, way, k)
                    part = rows_at(z + step * k)
                    v = own[at, part, :] + zl[slot, way, k - 2].astype(jnp.float32)
                    zs[slot, part, :] = v.astype(jnp.bfloat16)
                    (zr_copy if k == 2 else zl_copy)(slot, way, k).start()

    def z_total(slot, at):
        for way in range(2):
            count = z if way == 0 else Z - 1 - z
            count = jnp.where(direct(slot), count, jnp.minimum(count, 2))
            for k in range(1, Z):
                @pl.when(count == k)
                def _():
                    ref = zr.at[slot, way, 0:k]
                    copy(ref, ref, zr_s.at[way, 0], zr_r.at[slot, way], "dp", z_next).wait_recv()

            for k in range(1, Z):
                @pl.when(count >= k)
                def _():
                    own[at, mine, :] += zr[slot, way, k - 1].astype(jnp.float32)

    def columns(p):
        return slice(None) if C2 == 1 else pl.ds(pl.multiple_of(p * w2, w2), w2)

    NA = C2 - NB
    first = [(0, p) for p in range(NA)]
    if NB:
        rest = [(u, NA + b) for u in range(Y) for b in range(NB)] + [(1, p) for p in range(NA)]
    else:
        rest = [(u, p) for u in range(1, Y) for p in range(NA)]
    order = []
    if NB:
        while first or rest:
            order += first[:1] + rest[:1]
            first, rest = first[1:], rest[1:]
    else:
        order = first + rest
    steps = len(order)

    def chunk(i):
        i = jnp.clip(i, 0, steps - 1)
        return look([o[0] for o in order], i), look([o[1] for o in order], i)

    def slot_of(u, p):
        return jnp.where(u == Y - 1, p, p + NB)

    def scattered(u, p):
        return (u == Y - 1) | (p >= NA)

    def produce(i):
        u, p = chunk(i)
        at = u * C2 + p

        def one(j):
            n = 2 * u + 1 - j
            to = jnp.where(j == 0, Y * C2, at)
            own[to] = jnp.dot(hid[...], rv[n, :, columns(p)], preferred_element_type=jnp.float32)

            @pl.when(j == 0)
            def _():
                cs[at] = own[Y * C2].astype(jnp.bfloat16)
                cr_copy(at).start()

        loop(0, 2, one)

    def combine(i):
        u, p = chunk(i)
        at = u * C2 + p
        cr_copy(at).wait_recv()
        ringed = (u > 0) & (p < NA)
        for h in range(Z):
            if h == 3 and Z > 3:
                @pl.when(i == steps - 1)
                def _():
                    relay(steps - 2)

            part = rows_at(parts[h])
            own[at, part, :] += cr[at, part, :].astype(jnp.float32)

            @pl.when(ringed)
            def _():
                yr_copy(u, p, h).wait_recv()
                own[at, part, :] += yr[u - 1, p, part, :].astype(jnp.float32)

            @pl.when(scattered(u, p))
            def _():
                zs[slot_of(u, p), part, :] = own[at, part, :].astype(jnp.bfloat16)
                z_scatter(slot_of(u, p), parts[h])

            @pl.when(jnp.logical_not(scattered(u, p)))
            def _():
                ys[u, p, part, :] = own[at, part, :].astype(jnp.bfloat16)
                yr_copy(u + 1, p, h).start()

    def relay(i):
        u, p = chunk(i)

        @pl.when(scattered(u, p) & jnp.logical_not(direct(slot_of(u, p))))
        def _():
            z_relay(slot_of(u, p), u * C2 + p)

    def cross(b):
        at = NA + b
        z_total(C2 + b, at)
        yf[0, b] = own[at, mine, :].astype(jnp.bfloat16)
        yf_copy(b).start()

    def reduce(i):
        @pl.when(i == 0)
        def _():
            pltpu.make_async_copy(rv, rv, rsem).wait()

        @pl.when(i < steps)
        def _():
            produce(i)

        if Z > 3:
            @pl.when((i > 2) & (i != steps + 1))
            def _():
                relay(i - 3)

        @pl.when((i > 0) & (i <= steps))
        def _():
            combine(i - 1)

        for b in range(NB):
            @pl.when(i == steps)
            def _():
                cross(b)

    loop(0, steps + 3, reduce)

    last[...] = rbias[...][None, :]

    def drain():
        stats.wait_send()
        for way in range(2):
            step = 1 - 2 * way
            for d in range(1, Z):
                @pl.when(z_sends(way, d))
                def _():
                    ref = xg.at[0, :, rows_at(0), :]
                    copy(ref, ref, za_s.at[way, d - 1], za_r.at[way, 0, 0], "dp", z_next).wait_send()

                @pl.when(inside(z + step * d))
                def _():
                    ref = zs.at[:, rows_at(0), :]
                    copy(ref, ref, zr_s.at[way, d - 1], zr_r.at[0, way], "dp", z_next).wait_send()

        for u in range(Y):
            copy(xg.at[0], xg.at[0], ca_s.at[u], ca_r.at[u, 0], "tensor", t_part).wait_send()
        copy(cs, cr, cr_s, cr_r.at[0], "tensor", t_part).wait_send()
        for u in range(1, Y):
            ref = ys.at[u - 1, 0:NA]
            copy(xg.at[0], xg.at[0], ya_s.at[u - 1], ya_r.at[0, 0], "tensor", t_next).wait_send()
            copy(ref, ref, yr_s.at[u - 1], yr_r.at[0, 0, 0], "tensor", t_next).wait_send()
        for b in range(NB):
            yf_copy(b).wait_send()

    back = max(NA - 2, 0)
    turn = list(range(back)) + list(range(NA, C2)) + list(range(back, NA))

    def finish(i):
        @pl.when(i == C2 - 1)
        def _():
            drain()

        p = look(turn, i)
        at = (Y - 1) * C2 + p
        z_total(p, at)
        for b in range(NB):
            @pl.when(p == NA + b)
            def _():
                yf_copy(b).wait_recv()
                own[at, mine, :] += yf[1, b].astype(jnp.float32)

        cols = columns(p)
        add = own[at, mine, :] + last[:, cols]
        top = add.astype(jnp.bfloat16)
        rest = add - top.astype(jnp.float32)
        middle = rest.astype(jnp.bfloat16)
        low = (rest - middle.astype(jnp.float32)).astype(jnp.bfloat16)
        spread = jnp.dot(pick[...], low, preferred_element_type=jnp.float32)
        spread = spread + jnp.dot(pick[...], middle, preferred_element_type=jnp.float32)
        spread = spread + jnp.dot(pick[...], top, preferred_element_type=jnp.float32)
        pt[:, cols] = pt[:, cols] + spread

    loop(0, C2, finish)


def body(
    Z, T, patches, counts, ranking, norm_gain, expand_weight, expand_bias, reduce_weight, reduce_bias
):
    images, patch_len, dl = patches.shape
    hl, D = expand_weight.shape
    flat = patches.reshape(images * patch_len, dl)
    R, M, Y = CAP, Z * CAP, T // 2
    C = dl // 256 if dl % 256 == 0 else 1
    w2 = 256 if dl % 256 == 0 else dl
    C2 = dl // w2
    G = 2 if C % 2 == 0 else 1
    NB = 1 if Y == 2 and C2 > 4 else 0
    slots = C2 + NB
    dlc = dl // C
    vmem = pl.BlockSpec(memory_space=pltpu.VMEM)
    hbm = pl.BlockSpec(memory_space=pl.ANY)
    bf16, f32 = jnp.bfloat16, jnp.float32
    dma = pltpu.SemaphoreType.DMA
    N = images * patch_len
    smem = pl.BlockSpec(memory_space=pltpu.SMEM)
    result = pl.pallas_call(
        functools.partial(block_kernel, Z, T, C, G, C2, NB),
        out_shape=pltpu.VMEM((N, dl), f32),
        in_specs=[smem] * 2 + [vmem] * 4 + [hbm] * 3,
        out_specs=vmem,
        scratch_shapes=[
            pltpu.VMEM((R, dl), f32),
            pltpu.VMEM((N, R), bf16),
            pltpu.VMEM((T, C, M, dlc), bf16),
            pltpu.VMEM((T * C // G, hl, G * dlc), bf16),
            pltpu.VMEM((T, hl, dl), bf16),
            pltpu.VMEM((M, hl), f32),
            pltpu.VMEM((M, hl), bf16),
            pltpu.VMEM((1, dl), f32),
            pltpu.VMEM((T, 8, 2 * R), f32),
            pltpu.VMEM((Y * C2, M, w2), bf16),
            pltpu.VMEM((Y * C2, M, w2), bf16),
            pltpu.VMEM((Y * C2 + 1, M, w2), f32),
            pltpu.VMEM((Y - 1, C2, M, w2), bf16),
            pltpu.VMEM((Y - 1, C2, M, w2), bf16),
            pltpu.VMEM((slots, M, w2), bf16),
            pltpu.VMEM((slots, 2, Z - 1, R, w2), bf16),
            pltpu.VMEM((slots, 2, max(Z - 3, 1), R, w2), bf16),
            pltpu.VMEM((2, max(NB, 1), R, w2), bf16),
            dma, dma((C // G,)), dma, dma, dma,
            dma((2, Z - 1)), dma((2, Z - 1, C)),
            dma((Y - 1,)), dma((Y - 1, C // G)),
            dma((Y,)), dma((Y, C // G)),
            dma, dma((Y * C2,)),
            dma((Y - 1,)), dma((Y - 1, C2 - NB, Z)),
            dma((2, Z - 1)), dma((slots, 2)), dma((slots, 2, max(Z - 3, 1))),
            dma((max(NB, 1),)), dma((max(NB, 1),)),
        ],
        compiler_params=pltpu.CompilerParams(
            collective_id=0, has_side_effects=True, vmem_limit_bytes=63700000
        ),
        name="feed_forward",
    )(
        counts, ranking, ranking, norm_gain, expand_bias, reduce_bias, flat, expand_weight, reduce_weight,
    )
    return result.reshape(images, patch_len, dl)


def solution(mesh):
    placed = (
        P(("groups", "dp"), None, "tensor"),
        P(("groups", "dp")),
        P(("groups", "dp"), None),
        P("tensor"),
        P(("dp", "tensor"), None),
        P(("dp", "tensor")),
        P(("dp", "tensor"), None),
        P("tensor"),
    )
    return jax.shard_map(
        functools.partial(body, mesh.shape["dp"], mesh.shape["tensor"]),
        mesh=mesh,
        in_specs=placed,
        out_specs=P(("groups", "dp"), None, "tensor"),
        check_vma=False,
    )
```
